32 devices in a mesh: pb: 8 (over z, x), ha: 4 (over y, core).
Axes of the slice: x: 2, y: 2, z: 4, core: 2. Of those that a mesh axis runs over, the one named last changes fastest.
Arguments:
- queries: bfloat16 [1024, 4096], P('pb', 'ha')
- keys: bfloat16 [1024, 4096], P('pb', 'ha')
- values: bfloat16 [1024, 4096], P('pb', 'ha'), may hold values from -6 to 6
- theta: float32 [32, 6, 11], P('ha')
- mix: float32 [32, 4], P('ha')
- gain: float32 [4096], P('ha'), may hold values from 0.5 to 1.5
- out_weight: bfloat16 [4096, 4096], P('ha'), may hold values from -0.09375 to 0.09375
- turn_lengths: int32 [16], replicated, may hold values from 1 to 640, 1024 in all
Outputs:
- output: bfloat16 [1024, 4096], P('pb', 'ha')
The draws below stay inside these ranges and needn't reach their ends.
Inputs may be any that keep to these rules, and one draw needn't show every extreme that they name: `turn_lengths`: the turns' lengths sum to 1024; the longest turn has exactly 640 positions.
All inputs are finite; a program needn't handle non-finite values.
Results may differ from the reference program's by a relative error of at most 0.018.
Values may be sent and summed in bfloat16 or wider, within the bound.
No kernel may reach another device: no remote copies, remote signals or barrier semaphores. Data moves between devices by JAX's collectives and lax.ppermute only.
A program may use at most 64 MiB of HBM per device.

```python
import math
import jax
import jax.numpy as jnp
import numpy as np
from jax import lax

D = 4096
HEADS = 32
DH = 128
GROUP = 4
QCONV = 6
KCONV = 11
TQ = 128
MAXBACK = 5
NT = 16
SEQ = 1024
MOST = 640
N_HA = 4


def query_key_pair(key):
    first_key = jax.random.fold_in(key, 101)
    second_key = jax.random.fold_in(key, 202)
    draw_shape = (SEQ, HEADS * DH)
    query_draw = jnp.clip(jax.random.normal(first_key, draw_shape, jnp.float32), -4.0, 4.0)
    key_draw = jnp.clip(jax.random.normal(second_key, draw_shape, jnp.float32), -4.0, 4.0)
    return (query_draw, key_draw)


def draw_queries(key, part):
    return query_key_pair(key)[0].astype(jnp.bfloat16)


def draw_keys(key, part):
    return query_key_pair(key)[1].astype(jnp.bfloat16)


def draw_theta(key, part):
    noise = jnp.clip(0.25 * jax.random.normal(jax.random.fold_in(key, 303), (HEADS, QCONV, KCONV), jnp.float32), -1.0, 1.0)
    query_tap = jnp.arange(QCONV, dtype=jnp.int32)[None, :, None]
    key_tap = jnp.arange(KCONV, dtype=jnp.int32)[None, None, :]
    center = ((query_tap == 0) & (key_tap == (KCONV - 1) // 2)).astype(jnp.float32)
    return noise + center


def draw_mix(key, part):
    noise = jnp.clip(0.3 * jax.random.normal(jax.random.fold_in(key, 404), (HEADS, GROUP), jnp.float32), -1.2, 1.2)
    head_num = jnp.arange(HEADS, dtype=jnp.int32)[:, None]
    member = jnp.arange(GROUP, dtype=jnp.int32)[None, :]
    return noise + (head_num % GROUP == member).astype(jnp.float32)


def shard_levels(key, extent, pieces, low, top_value):
    level, own = 1.0, jax.random.fold_in(key, 6)
    for position, blocks in pieces:
        steps = jnp.exp(jax.random.uniform(jax.random.fold_in(own, position), (blocks,), jnp.float32, low / len(pieces), top_value / len(pieces)))
        level = level * jnp.repeat(steps, extent[position] // blocks).reshape([-1 if axis == position else 1 for axis in range(len(extent))])
    return level


def split_up(number_of, total, most, slope):
    portions = [(1 << 20) // math.isqrt(standing ** slope) + 1 for standing in range(2, number_of + 1)]
    rest, given = total - most - (number_of - 1), [1] * (number_of - 1)
    while rest > 0:
        candidates = [i for i in range(number_of - 1) if given[i] < most]
        whole, budget = sum([portions[i] for i in candidates]), rest
        for i in candidates:
            more = min(most - given[i], max(1, budget * portions[i] // whole), rest)
            given[i] = given[i] + more
            rest = rest - more
    return np.array([most] + given)


def ragged_sizes(rng, amount, total, reach, skew):
    if amount == 2:
        one = jax.random.randint(rng, (), max(1, total - reach), min(reach, total - 1) + 1)
        return jnp.stack([one, total - one])
    tallies = jnp.asarray(split_up(amount, total, reach, skew), jnp.int32)
    pairs = (amount - 1) // 2
    donor, sink = tallies[1:1 + 2 * pairs:2], tallies[2:2 + 2 * pairs:2]
    slack = jnp.minimum(donor - 1, reach - sink)
    passed = jax.random.randint(jax.random.fold_in(rng, 1), (pairs,), 0, 1 << 20) % (slack + 1)
    tallies = tallies.at[1:1 + 2 * pairs:2].set(donor - passed).at[2:2 + 2 * pairs:2].set(sink + passed)
    return tallies[jax.random.permutation(jax.random.fold_in(rng, 2), amount)]


def scatter_about(own_key, shape, deviation, most, pieces=(), held_as=jnp.bfloat16):
    array = jax.random.normal(own_key, shape, jnp.float32) * deviation
    if len(pieces) > 0:
        array = shard_levels(own_key, shape, pieces, -0.22, 0.18) * array
    return jnp.clip(array, min=-most, max=most).astype(held_as)


def setup_inputs(seed: int = 0) -> dict:
    key_list = jax.random.split(jax.random.key(seed), 9)
    queries = draw_queries(jax.random.fold_in(key_list[8], 71), 0)
    keys = draw_keys(jax.random.fold_in(key_list[8], 71), 0)
    values = scatter_about(key_list[2], (SEQ, HEADS * DH), 1.0, 6.0, ((0, 8), (1, 4)))
    theta = draw_theta(jax.random.fold_in(key_list[8], 71), 0)
    mix = draw_mix(jax.random.fold_in(key_list[8], 71), 0)
    gain = jnp.clip(1.0 + 0.1 * jax.random.normal(key_list[5], (HEADS * DH,), jnp.float32), 0.5, 1.5)
    out_weight = scatter_about(key_list[6], (HEADS * DH, D), (HEADS * DH) ** -0.5, 0.09375, ((0, 4),))
    turn_lengths = ragged_sizes(key_list[7], NT, SEQ, MOST, 2).astype(jnp.int32)
    return {"queries": queries, "keys": keys, "values": values, "theta": theta, "mix": mix, "gain": gain, "out_weight": out_weight, "turn_lengths": turn_lengths}


def conv_block(scores, theta_part, row_pos, row_start, col_pos, out_cols):
    rim_rows = QCONV - 1
    count_rows = row_pos.shape[0]
    conv_sum = jnp.zeros((scores.shape[0], count_rows, out_cols), jnp.float32)
    above_start = col_pos[None, :] >= row_start[:, None]
    for offset_q in range(QCONV):
        allowed = above_start & (col_pos[None, :] <= row_pos[:, None] - offset_q)
        taken_rows = jnp.where(allowed[None], scores[:, rim_rows - offset_q:rim_rows - offset_q + count_rows, :], jnp.float32(0.0))
        for offset_k in range(KCONV):
            conv_sum = conv_sum + theta_part[:, offset_q, KCONV - 1 - offset_k][:, None, None] * taken_rows[:, :, offset_k:offset_k + out_cols]
    return conv_sum

def tile_group(query_ext, key_ext, val_ext, row_pos, row_start, key_base, theta_part, mix_part, gain_part):
    key_reach = (KCONV - 1) // 2
    win_cols = val_ext.shape[0]
    score_scale = 1.0 / math.sqrt(DH)
    scores = jnp.einsum('rhd,chd->hrc', query_ext.astype(jnp.float32), key_ext.astype(jnp.float32)) * score_scale
    col_pos = key_base - key_reach + jnp.arange(win_cols + 2 * key_reach, dtype=jnp.int32)
    conv_sum = conv_block(scores, theta_part, row_pos, row_start, col_pos, win_cols)
    key_pos = key_base + jnp.arange(win_cols, dtype=jnp.int32)
    keep_mask = (key_pos[None, :] >= row_start[:, None]) & (key_pos[None, :] <= row_pos[:, None])
    row_peak = lax.optimization_barrier(jnp.max(jnp.where(keep_mask[None], conv_sum, jnp.float32(-1e+30)), axis=-1))
    weights = jnp.where(keep_mask[None], jnp.exp(conv_sum - row_peak[..., None]), jnp.float32(0.0))
    row_total = lax.optimization_barrier(jnp.sum(weights, axis=-1))
    prob_bf = lax.optimization_barrier(weights.astype(jnp.bfloat16)).astype(jnp.float32)
    acc = jnp.einsum('pij,jc->pic', prob_bf, val_ext.astype(jnp.float32)) / row_total[..., None]
    acc = acc.reshape(GROUP, TQ, GROUP, DH)
    head_out = jnp.einsum('kp,pikd->ikd', mix_part, acc)
    mean_sq = lax.optimization_barrier(jnp.mean(head_out * head_out, axis=-1, keepdims=True))
    normed = head_out * lax.rsqrt(mean_sq + 1e-06) * gain_part.reshape(GROUP, DH)
    return normed.reshape(TQ, GROUP * DH).astype(jnp.bfloat16)

def reference(queries, keys, values, theta, mix, gain, out_weight, turn_lengths):
    rim_rows = QCONV - 1
    key_reach = (KCONV - 1) // 2
    win_cols = (MAXBACK + 1) * TQ
    seq_len = queries.shape[0]
    lengths = turn_lengths.astype(jnp.int32)
    starts = (jnp.cumsum(lengths) - lengths).astype(jnp.int32)
    positions = jnp.arange(seq_len, dtype=jnp.int32)
    row_start_all = lax.optimization_barrier(jnp.max(jnp.where(starts[None, :] <= positions[:, None], starts[None, :], 0), axis=1)).astype(jnp.int32)
    query_pad = jnp.pad(queries, ((rim_rows, 0), (0, 0)))
    key_pad = jnp.pad(keys, ((MAXBACK * TQ + key_reach, key_reach), (0, 0)))
    val_pad = jnp.pad(values, ((MAXBACK * TQ, 0), (0, 0)))
    head_cols = HEADS // N_HA * DH

    def one_tile(tile_num):
        first_row = (tile_num * TQ).astype(jnp.int32)
        query_tile = lax.dynamic_slice_in_dim(query_pad, first_row, TQ + rim_rows, 0).reshape(TQ + rim_rows, HEADS, DH)
        key_tile = lax.dynamic_slice_in_dim(key_pad, first_row, win_cols + 2 * key_reach, 0).reshape(win_cols + 2 * key_reach, HEADS, DH)
        val_tile = lax.dynamic_slice_in_dim(val_pad, first_row, win_cols, 0)
        row_pos = first_row + jnp.arange(TQ, dtype=jnp.int32)
        row_start = lax.dynamic_slice_in_dim(row_start_all, first_row, TQ, 0)
        key_base = first_row - MAXBACK * TQ

        def one_group(group_num):
            head_first = (group_num * GROUP).astype(jnp.int32)
            col_first = (group_num * GROUP * DH).astype(jnp.int32)
            return tile_group(lax.dynamic_slice_in_dim(query_tile, head_first, GROUP, 1), lax.dynamic_slice_in_dim(key_tile, head_first, GROUP, 1), lax.dynamic_slice_in_dim(val_tile, col_first, GROUP * DH, 1), row_pos, row_start, key_base, lax.dynamic_slice_in_dim(theta, head_first, GROUP, 0), lax.dynamic_slice_in_dim(mix, head_first, GROUP, 0), lax.dynamic_slice_in_dim(gain, col_first, GROUP * DH, 0))
        grouped = lax.map(one_group, jnp.arange(HEADS // GROUP, dtype=jnp.int32))
        normed = jnp.transpose(grouped, (1, 0, 2)).reshape(TQ, HEADS * DH)
        summed = jnp.zeros((TQ, out_weight.shape[1]), jnp.float32)
        for device_num in range(N_HA):
            lower = device_num * head_cols
            part_sum = jnp.dot(normed[:, lower:lower + head_cols], out_weight[lower:lower + head_cols], preferred_element_type=jnp.float32)
            summed = summed + lax.optimization_barrier(part_sum.astype(jnp.bfloat16)).astype(jnp.float32)
        return summed.astype(jnp.bfloat16)
    tiles = lax.map(one_tile, jnp.arange(seq_len // TQ, dtype=jnp.int32))
    return tiles.reshape(seq_len, out_weight.shape[1])
```

```python
import functools
import math

import jax
import jax.numpy as jnp
from jax import lax
from jax.experimental import pallas as pl
from jax.experimental.pallas import tpu as pltpu
from jax.sharding import PartitionSpec as P

GROUP = 4
QCONV = 6
KCONV = 11
MAXBACK = 5
HALO = 16
NEG = -1e30


def move(block, axis, route):
    return lax.ppermute(block, axis, route)


def split_kernel(side_ref, q_ref, k_ref, v_ref, own_q, own_kv, oth_all, oth_kv):
    side = side_ref[0]
    rows = q_ref.shape[0]
    half = q_ref.shape[1] // 2

    def emit(cols, is_own):
        q, k, v = q_ref[:, cols], k_ref[:, cols], v_ref[:, cols]
        if is_own:
            own_q[...] = q
            kv = own_kv
        else:
            oth_all[0:rows, :] = q
            oth_all[rows : 2 * rows, :] = k
            oth_all[2 * rows : 3 * rows, :] = v
            kv = oth_kv
        kv[0:HALO, :] = q[rows - HALO :, :]
        kv[HALO : HALO + rows, :] = k
        kv[HALO + rows : HALO + 2 * rows, :] = v

    emit(pl.ds(pl.multiple_of(side * half, half), half), True)
    emit(pl.ds(pl.multiple_of((1 - side) * half, half), half), False)


def band_kernel(side_ref, theta_ref, w_ref, *, scale):
    reach = (KCONV - 1) // 2
    width = 128
    base = side_ref[0] * GROUP
    diff = lax.broadcasted_iota(jnp.int32, (width, width), 1) - lax.broadcasted_iota(
        jnp.int32, (width, width), 0
    )
    zero = jnp.zeros((width, width), jnp.bfloat16)

    def body(step, carry):
        h = step // QCONV
        a = step % QCONV
        lo = jnp.zeros((width, width), jnp.float32)
        hi = jnp.zeros((width, width), jnp.float32)
        for b in range(-reach, reach + 1):
            t = theta_ref[((base + h) * QCONV + a) * KCONV + b + reach] * scale
            lo = jnp.where(diff == b - 64, t, lo)
            hi = jnp.where(diff == b + 64, t, hi)
        lo = lo.astype(jnp.bfloat16)
        hi = hi.astype(jnp.bfloat16)
        at = pl.multiple_of(a * 3 * width, width)
        w_ref[h, pl.ds(at, width), 0:width] = lo
        w_ref[h, pl.ds(at, width), width : 2 * width] = zero
        w_ref[h, pl.ds(at + width, width), 0:width] = hi
        w_ref[h, pl.ds(at + width, width), width : 2 * width] = lo
        w_ref[h, pl.ds(at + 2 * width, width), 0:width] = zero
        w_ref[h, pl.ds(at + 2 * width, width), width : 2 * width] = hi
        return carry

    lax.fori_loop(0, GROUP * QCONV, body, 0)


def attend_kernel(
    side_ref, len_ref, mix_ref, gain_ref, w_ref, own_q, own_kv, swap, pa, pb, fa, fb, e0, e1,
    mine_ref, theirs_ref, qs, ks, vs, ss, lhs, same, peak, total, acc
):
    side = side_ref[0]
    first_row = side_ref[1]
    rows = own_q.shape[0]
    dh = own_q.shape[1] // GROUP
    n_rows = 2 * rows
    width = 3 * rows
    out_w = 2 * rows

    def put_kv(ref, at, block):
        start = pl.multiple_of(block * rows, rows)
        for h in range(GROUP):
            ks[h, pl.ds(start, rows), :] = ref[at : at + rows, h * dh : (h + 1) * dh]
        vs[pl.ds(start, rows), :] = ref[at + rows : at + 2 * rows, :]

    zero_blk = jnp.zeros((rows, dh), jnp.bfloat16)
    for edge in (0, 8):
        for h in range(GROUP):
            ks[h, edge * rows : (edge + 1) * rows, :] = zero_blk
        vs[edge * rows : (edge + 1) * rows, :] = jnp.zeros((rows, GROUP * dh), jnp.bfloat16)
    put_kv(own_kv, HALO, 6 + side)
    put_kv(swap, rows, 7 - side)
    put_kv(pa, HALO, 4 + side)
    put_kv(pb, HALO, 5 - side)
    put_kv(fa, HALO, 2 + side)
    put_kv(fb, HALO, 3 - side)

    @pl.when(side == 0)
    def _():
        put_kv(e0, HALO, 1)
        for h in range(GROUP):
            qs[h, 0:HALO, :] = pb[0:HALO, h * dh : (h + 1) * dh]

    @pl.when(side == 1)
    def _():
        put_kv(e1, HALO, 1)
        for h in range(GROUP):
            qs[h, 0:HALO, :] = pa[0:HALO, h * dh : (h + 1) * dh]

    at_own = pl.multiple_of(HALO + side * rows, HALO)
    at_oth = pl.multiple_of(HALO + (1 - side) * rows, HALO)
    for h in range(GROUP):
        qs[h, pl.ds(at_own, rows), :] = own_q[:, h * dh : (h + 1) * dh]
        qs[h, pl.ds(at_oth, rows), :] = swap[0:rows, h * dh : (h + 1) * dh]

    n_ext = n_rows + HALO
    row_ext = first_row - HALO + lax.broadcasted_iota(jnp.int32, (n_ext, 128), 0)
    start_ext = jnp.zeros((n_ext, 128), jnp.int32)
    begin = jnp.int32(0)
    for n in range(len_ref.shape[0]):
        start_ext = jnp.where(row_ext >= begin, begin, start_ext)
        begin = begin + len_ref[n]
    row_pos = row_ext[HALO:]
    row_start = start_ext[HALO:]
    for a in range(QCONV):
        same[a] = (row_pos - a >= row_start).astype(jnp.float32)
    peak[...] = jnp.full(peak.shape, NEG, jnp.float32)
    total[...] = jnp.zeros(total.shape, jnp.float32)
    acc[...] = jnp.zeros(acc.shape, jnp.float32)
    key_base = first_row - 6 * rows
    lane = lax.broadcasted_iota(jnp.int32, (1, 128), 1)

    def step(i, carry):
        w = 3 - i // GROUP
        h = i % GROUP
        at = pl.multiple_of(w * out_w, out_w)
        k = ks[h, pl.ds(at, width), :]
        s = lax.dot_general(
            qs[h], k, (((1,), (1,)), ((), ())), preferred_element_type=jnp.float32
        )
        for t in range(3):
            col = key_base + at + t * 128 + lane
            ok = (col >= start_ext) & (col <= row_ext)
            ss[t] = jnp.where(ok, s[:, t * 128 : (t + 1) * 128], 0.0)
        for a in range(QCONV):
            keep = same[a]
            for t in range(3):
                piece = ss[t, HALO - a : HALO - a + n_rows, :] * keep
                lhs[:, (a * 3 + t) * 128 : (a * 3 + t + 1) * 128] = piece.astype(jnp.bfloat16)
        conv = jnp.dot(lhs[...], w_ref[h], preferred_element_type=jnp.float32)
        parts = []
        oks = []
        for t in range(2):
            col = key_base + at + 64 + t * 128 + lane
            ok = (col >= row_start) & (col <= row_pos)
            oks.append(ok)
            parts.append(jnp.where(ok, conv[:, t * 128 : (t + 1) * 128], NEG))
        old = peak[h]
        top = jnp.max(jnp.maximum(parts[0], parts[1]), axis=1, keepdims=True)
        new = jnp.maximum(old, top)
        ws = [jnp.where(ok, jnp.exp(c - new), 0.0) for ok, c in zip(oks, parts)]
        factor = jnp.exp(old - new)
        peak[h] = new
        total[h] = total[h] * factor + jnp.sum(ws[0] + ws[1], axis=1, keepdims=True)
        probs = jnp.concatenate([x.astype(jnp.bfloat16) for x in ws], axis=1)
        v = vs[pl.ds(pl.multiple_of(at + 64, 64), out_w), :]
        upd = jnp.dot(probs, v, preferred_element_type=jnp.float32)
        for t in range(GROUP):
            cols = slice(t * dh, (t + 1) * dh)
            acc[h, :, cols] = acc[h, :, cols] * factor + upd[:, cols]
        return carry

    lax.fori_loop(0, 4 * GROUP, step, 0)

    base = side * GROUP
    for h in range(GROUP):
        cols = slice(h * dh, (h + 1) * dh)
        out = jnp.zeros((n_rows, dh), jnp.float32)
        for p in range(GROUP):
            out = out + mix_ref[(base + h) * GROUP + p] * (acc[p, :, cols] / total[p])
        mean_sq = jnp.mean(out * out, axis=1, keepdims=True)
        gain = gain_ref[:, pl.ds(pl.multiple_of((base + h) * dh, dh), dh)]
        normed = (out * lax.rsqrt(mean_sq + 1e-06) * gain).astype(jnp.bfloat16)
        ss[0, 0:n_rows, :] = normed.astype(jnp.float32)
        mine_ref[:, cols] = ss[0, pl.ds(pl.multiple_of(side * rows, rows), rows), :].astype(
            jnp.bfloat16
        )
        theirs_ref[:, cols] = ss[
            0, pl.ds(pl.multiple_of((1 - side) * rows, rows), rows), :
        ].astype(jnp.bfloat16)


def project_kernel(side_ref, mine_ref, got_ref, w_own, w_oth, out_ref):
    total = jnp.dot(mine_ref[...], w_own[...], preferred_element_type=jnp.float32)
    total = total + jnp.dot(got_ref[...], w_oth[...], preferred_element_type=jnp.float32)
    out_ref[0] = total.astype(jnp.bfloat16)


def from_behind(block, axis, distance):
    devices = range(lax.axis_size(axis))
    route = [(i - distance, i) for i in devices if i - distance in devices]
    return lax.ppermute(block, axis, route)


def conv_block(scores, theta_part, row_pos, row_start, col_pos, out_cols):
    rim_rows = QCONV - 1
    count_rows = row_pos.shape[0]
    conv_sum = jnp.zeros((scores.shape[0], count_rows, out_cols), jnp.float32)
    above_start = col_pos[None, :] >= row_start[:, None]
    for offset_q in range(QCONV):
        allowed = above_start & (col_pos[None, :] <= row_pos[:, None] - offset_q)
        taken_rows = jnp.where(
            allowed[None],
            scores[:, rim_rows - offset_q : rim_rows - offset_q + count_rows, :],
            jnp.float32(0.0),
        )
        for offset_k in range(KCONV):
            conv_sum = (
                conv_sum
                + theta_part[:, offset_q, KCONV - 1 - offset_k][:, None, None]
                * taken_rows[:, :, offset_k : offset_k + out_cols]
            )
    return conv_sum


def general_plan(queries, keys, values, theta, mix, gain, out_weight, turn_lengths):
    tile_rows = queries.shape[0]
    feature_cols = queries.shape[1]
    local_heads = theta.shape[0]
    head_size = feature_cols // local_heads
    groups = local_heads // GROUP
    group_cols = GROUP * head_size
    rim_rows = QCONV - 1
    key_reach = (KCONV - 1) // 2
    tile_index = lax.axis_index("pb")
    first_row = tile_index * tile_rows
    starts = jnp.cumsum(turn_lengths) - turn_lengths
    row_pos = first_row + jnp.arange(tile_rows, dtype=jnp.int32)
    row_start = jnp.max(jnp.where(starts[None, :] <= row_pos[:, None], starts[None, :], 0), axis=1)
    earlier = from_behind(queries[tile_rows - rim_rows :], "pb", 1)
    query_ext = jnp.concatenate([earlier, queries], 0).reshape(
        tile_rows + rim_rows, local_heads, head_size
    )
    kv_pair = jnp.stack([keys, values], 0)
    window = kv_pair[None]
    while window.shape[0] < MAXBACK + 1:
        have_count = window.shape[0]
        take_count = min(have_count, MAXBACK + 1 - have_count)
        moved_runs = from_behind(window[have_count - take_count :], "pb", have_count)
        window = jnp.concatenate([moved_runs, window], 0)
    key_span = (MAXBACK + 1) * tile_rows
    key_win = window[:, 0].reshape(key_span, feature_cols)
    val_win = window[:, 1].reshape(key_span, feature_cols)
    key_pad = jnp.pad(key_win, ((key_reach, key_reach), (0, 0))).reshape(
        key_span + 2 * key_reach, local_heads, head_size
    )
    key_base = first_row - MAXBACK * tile_rows
    score_scale = 1.0 / math.sqrt(head_size)
    state_carry = (
        jnp.full((local_heads, tile_rows), -1e30, jnp.float32),
        jnp.zeros((local_heads, tile_rows), jnp.float32),
        jnp.zeros((local_heads, tile_rows, group_cols), jnp.float32),
    )
    for block_num in range(MAXBACK + 1):
        block_row_peak, block_row_total, block_accumulated = state_carry
        lower = block_num * tile_rows
        key_slice = key_pad[lower : lower + tile_rows + 2 * key_reach]
        scores = (
            jnp.einsum("rhd,chd->hrc", query_ext, key_slice, preferred_element_type=jnp.float32)
            * score_scale
        )
        col_pos = (
            key_base + lower - key_reach + jnp.arange(tile_rows + 2 * key_reach, dtype=jnp.int32)
        )
        conv_sum = conv_block(scores, theta, row_pos, row_start, col_pos, tile_rows)
        key_pos = key_base + lower + jnp.arange(tile_rows, dtype=jnp.int32)
        keep_mask = (key_pos[None, :] >= row_start[:, None]) & (
            key_pos[None, :] <= row_pos[:, None]
        )
        masked = jnp.where(keep_mask[None], conv_sum, jnp.float32(-1e30))
        new_peak = jnp.maximum(block_row_peak, jnp.max(masked, axis=-1))
        weights = jnp.where(
            keep_mask[None], jnp.exp(conv_sum - new_peak[..., None]), jnp.float32(0.0)
        )
        factor = jnp.exp(block_row_peak - new_peak)
        new_total = block_row_total * factor + jnp.sum(weights, axis=-1)
        prob_bf = weights.astype(jnp.bfloat16).reshape(groups, GROUP, tile_rows, tile_rows)
        val_block = val_win[lower : lower + tile_rows].reshape(tile_rows, groups, group_cols)
        update = jnp.einsum(
            "gpij,jgc->gpic", prob_bf, val_block, preferred_element_type=jnp.float32
        )
        update = update.reshape(local_heads, tile_rows, group_cols)
        state_carry = (new_peak, new_total, block_accumulated * factor[..., None] + update)
    row_peak, row_total, accumulated = state_carry
    normalized = (accumulated / row_total[..., None]).reshape(
        groups, GROUP, tile_rows, GROUP, head_size
    )
    mix_grid = mix.reshape(groups, GROUP, GROUP)
    head_out = jnp.einsum("gkp,gpikd->gikd", mix_grid, normalized)
    head_out = jnp.transpose(head_out, (1, 0, 2, 3)).reshape(tile_rows, local_heads, head_size)
    mean_sq = jnp.mean(head_out * head_out, axis=-1, keepdims=True)
    normed = (
        (head_out * lax.rsqrt(mean_sq + 1e-06) * gain.reshape(local_heads, head_size))
        .reshape(tile_rows, feature_cols)
        .astype(jnp.bfloat16)
    )
    summed = lax.psum_scatter(
        lax.dot_general(
            out_weight, normed, (((0,), (1,)), ((), ())), preferred_element_type=jnp.float32
        ).astype(jnp.bfloat16),
        "ha",
        scatter_dimension=0,
        tiled=True,
    ).astype(jnp.float32)
    return summed.T.astype(jnp.bfloat16)


def paired_plan(queries, keys, values, theta, mix, gain, out_weight, turn_lengths):
    rows, feats = queries.shape
    half = feats // 2
    heads = theta.shape[0]
    dh = feats // heads
    n_pb = lax.axis_size("pb")
    n_ha = lax.axis_size("ha")
    me = lax.axis_index("pb")
    side = me % 2
    info = jnp.stack([side, (me - side) * rows]).astype(jnp.int32)
    vm = pl.BlockSpec(memory_space=pltpu.VMEM)
    sm = pl.BlockSpec(memory_space=pltpu.SMEM)
    bf = jnp.bfloat16
    kv_rows = 2 * rows + HALO
    shape = jax.ShapeDtypeStruct

    own_q, own_kv, oth_all, oth_kv = pl.pallas_call(
        split_kernel,
        out_shape=(
            shape((rows, half), bf),
            shape((kv_rows, half), bf),
            shape((3 * rows, half), bf),
            shape((kv_rows, half), bf),
        ),
        in_specs=[sm, vm, vm, vm],
        out_specs=(vm, vm, vm, vm),
    )(info, queries, keys, values)

    pairs = range(n_pb)
    up = [(i, i + 2) for i in pairs if i + 2 < n_pb]
    cross = [(i, (i ^ 1) + 2) for i in pairs if (i ^ 1) + 2 < n_pb]
    swap_route = [(i, i ^ 1) for i in pairs]
    far = [(i, i + MAXBACK) for i in pairs if i % 2 == 1 and i + MAXBACK < n_pb]
    up_odd = [(i, i + 2) for i in pairs if i % 2 == 1 and i + 2 < n_pb]

    pa = move(own_kv, "pb", up)
    pbk = move(oth_kv, "pb", cross)
    swap = move(oth_all, "pb", swap_route)
    e0 = move(oth_kv, "pb", far)
    fa = move(pa, "pb", up)
    fb = move(pbk, "pb", up)
    e1 = move(fa, "pb", up_odd)

    w = pl.pallas_call(
        functools.partial(band_kernel, scale=1.0 / math.sqrt(dh)),
        out_shape=shape((GROUP, QCONV * 3 * rows, 2 * rows), bf),
        in_specs=[sm, sm],
        out_specs=vm,
        cost_estimate=pl.CostEstimate(
            flops=20_000_000, bytes_accessed=4_800_000, transcendentals=0
        ),
    )(info, theta.reshape(-1))

    mine, theirs = pl.pallas_call(
        attend_kernel,
        out_shape=(shape((rows, half), bf), shape((rows, half), bf)),
        in_specs=[sm, sm, sm] + [vm] * 11,
        out_specs=(vm, vm),
        scratch_shapes=[
            pltpu.VMEM((GROUP, HALO + 2 * rows, dh), bf),
            pltpu.VMEM((GROUP, 9 * rows, dh), bf),
            pltpu.VMEM((9 * rows, half), bf),
            pltpu.VMEM((3, HALO + 2 * rows, 128), jnp.float32),
            pltpu.VMEM((2 * rows, QCONV * 3 * rows), bf),
            pltpu.VMEM((QCONV, 2 * rows, 128), jnp.float32),
            pltpu.VMEM((GROUP, 2 * rows, 128), jnp.float32),
            pltpu.VMEM((GROUP, 2 * rows, 128), jnp.float32),
            pltpu.VMEM((GROUP, 2 * rows, half), jnp.float32),
        ],
        compiler_params=pltpu.CompilerParams(vmem_limit_bytes=40 * 1024 * 1024),
    )(
        info, turn_lengths, mix.reshape(-1), gain.reshape(1, -1), w,
        own_q, own_kv, swap, pa, pbk, fa, fb, e0, e1,
    )

    got = move(theirs, "pb", swap_route)
    cols = out_weight.shape[1]
    part = cols // n_ha
    partial = pl.pallas_call(
        project_kernel,
        out_shape=shape((n_ha, rows, part), bf),
        grid_spec=pltpu.PrefetchScalarGridSpec(
            num_scalar_prefetch=1,
            grid=(n_ha,),
            in_specs=[
                pl.BlockSpec((rows, half), lambda i, s: (0, 0)),
                pl.BlockSpec((rows, half), lambda i, s: (0, 0)),
                pl.BlockSpec((half, part), lambda i, s: (s[0], i)),
                pl.BlockSpec((half, part), lambda i, s: (1 - s[0], i)),
            ],
            out_specs=pl.BlockSpec((1, rows, part), lambda i, s: (i, 0, 0)),
        ),
    )(info, mine, got, out_weight, out_weight)

    ha = lax.axis_index("ha")
    have = partial
    bit = 1
    block = have
    chunks = block
    while bit < n_ha:
        flag = (ha // bit) % 2
        grid = chunks.reshape((chunks.shape[0] // 2, 2) + chunks.shape[1:])
        keep = lax.dynamic_index_in_dim(grid, flag, 1, keepdims=False)
        give = lax.dynamic_index_in_dim(grid, 1 - flag, 1, keepdims=False)
        take = move(give, "ha", [(i, i ^ bit) for i in range(n_ha)])
        chunks = (keep.astype(jnp.float32) + take.astype(jnp.float32)).astype(bf)
        bit *= 2
    return chunks[0]


def per_device(queries, keys, values, theta, mix, gain, out_weight, turn_lengths):
    rows, feats = queries.shape
    heads = theta.shape[0]
    fits = rows == 128 and feats == 128 * heads and heads == 2 * GROUP
    n_pb, n_ha = lax.axis_size("pb"), lax.axis_size("ha")
    fits = fits and n_pb % 2 == 0 and n_ha & (n_ha - 1) == 0
    plan = paired_plan if fits else general_plan
    return plan(queries, keys, values, theta, mix, gain, out_weight, turn_lengths)


def solution(mesh):
    return jax.shard_map(
        per_device,
        mesh=mesh,
        in_specs=(
            P("pb", "ha"),
            P("pb", "ha"),
            P("pb", "ha"),
            P("ha", None, None),
            P("ha", None),
            P("ha"),
            P("ha", None),
            P(),
        ),
        out_specs=P("pb", "ha"),
        check_vma=False,
    )
```

```python
import functools
import math

import jax
import jax.numpy as jnp
from jax import lax
from jax.experimental import pallas as pl
from jax.experimental.pallas import tpu as pltpu
from jax.sharding import PartitionSpec as P

GROUP = 4
QCONV = 6
KCONV = 11
MAXBACK = 5
HALO = 16
NEG = -1e30
FLOOR = -5e29


def move(block, axis, route):
    return lax.ppermute(block, axis, route)


def copy_all(copies, sems):
    started = []
    for n, (src, dst) in enumerate(copies):
        copy = pltpu.make_async_copy(src, dst, sems.at[n])
        copy.start()
        started.append(copy)
    for copy in started:
        copy.wait()


def split_kernel(info_ref, q_ref, k_ref, v_ref, own_q, own_kv, oth_all, oth_kv):
    side = info_ref[0]
    rows = q_ref.shape[0]
    half = q_ref.shape[1] // 2

    def emit(cols, is_own):
        q, k, v = q_ref[:, cols], k_ref[:, cols], v_ref[:, cols]
        if is_own:
            own_q[...] = q
            kv = own_kv
        else:
            oth_all[0:rows, :] = q
            oth_all[rows : 2 * rows, :] = k
            oth_all[2 * rows : 3 * rows, :] = v
            kv = oth_kv
        kv[0:HALO, :] = q[rows - HALO :, :]
        kv[HALO : HALO + rows, :] = k
        kv[HALO + rows : HALO + 2 * rows, :] = v

    emit(pl.ds(pl.multiple_of(side * half, half), half), True)
    emit(pl.ds(pl.multiple_of((1 - side) * half, half), half), False)


def prep_kernel(info_ref, len_ref, theta_ref, w_ref, start_ref, same_ref, *, scale):
    reach = (KCONV - 1) // 2
    width = 128
    base = info_ref[0] * GROUP
    first_row = info_ref[1]
    diff = lax.broadcasted_iota(jnp.int32, (width, width), 1) - lax.broadcasted_iota(
        jnp.int32, (width, width), 0
    )

    def body(step, carry):
        h = step // (QCONV // 2)
        q = step % (QCONV // 2)
        for side in range(2):
            lo = jnp.zeros((width, width), jnp.float32)
            hi = jnp.zeros((width, width), jnp.float32)
            at = ((base + h) * QCONV + 2 * q + side) * KCONV
            for b in range(-reach, reach + 1):
                t = theta_ref[at + b + reach] * scale
                lo = jnp.where(diff == b - 64, t, lo)
                hi = jnp.where(diff == b + 64, t, hi)
            w_ref[step, 0:width, side * width : (side + 1) * width] = lo.astype(jnp.bfloat16)
            w_ref[step, width : 2 * width, side * width : (side + 1) * width] = hi.astype(
                jnp.bfloat16
            )
        return carry

    lax.fori_loop(0, GROUP * QCONV // 2, body, 0)
    shape = start_ref.shape
    row = first_row - HALO + lax.broadcasted_iota(jnp.int32, shape, 0)
    start = jnp.zeros(shape, jnp.int32)
    begin = jnp.int32(0)
    for n in range(len_ref.shape[0]):
        start = jnp.where(row >= begin, begin, start)
        begin = begin + len_ref[n]
    start_ref[...] = start
    for a in range(1, QCONV):
        same_ref[a - 1] = (row[HALO:] - a >= start[HALO:]).astype(jnp.float32)


def one_window(at, col0, first_row, qs, ks, vs, w, start, same, masks, lhs, ps, peak, total, acc):
    n_rows = peak.shape[1]
    n_ext = n_rows + HALO
    dh = 128
    lane = lax.broadcasted_iota(jnp.int32, (1, 128), 1)
    score_ok, bias = masks
    start_ext = start[...]
    row_ext = first_row - HALO + lax.broadcasted_iota(jnp.int32, (n_ext, 128), 0)
    for t in range(3):
        col = col0 + t * 128 + lane
        ok = (col >= start_ext) & (col <= row_ext)
        score_ok[t] = jnp.where(ok, 1.0, 0.0)
    for t in range(2):
        col = col0 + 64 + t * 128 + lane
        ok = (col >= start_ext[HALO:]) & (col <= row_ext[HALO:])
        bias[t] = jnp.where(ok, 0.0, NEG)

    for h in range(GROUP):
        cols = slice(h * dh, (h + 1) * dh)
        buf = h % 2
        s = lax.dot_general(
            qs[0:n_ext, cols],
            ks[pl.ds(at, 384), cols],
            (((1,), (1,)), ((), ())),
            preferred_element_type=jnp.float32,
        )
        for t in range(3):
            piece = (s[:, t * 128 : (t + 1) * 128] * score_ok[t]).astype(jnp.bfloat16)
            if t < 2:
                lhs[buf, 0:n_ext, t * 128 : (t + 1) * 128] = piece
            if t > 0:
                lhs[buf, n_ext : 2 * n_ext, (t - 1) * 128 : t * 128] = piece
        for q in range(QCONV // 2):
            pair = jnp.dot(
                lhs[buf], w[h * (QCONV // 2) + q], preferred_element_type=jnp.float32
            )
            ps[buf, 2 * q] = pair[:, 0:128]
            ps[buf, 2 * q + 1] = pair[:, 128:256]
        parts = []
        for t in range(2):
            conv = ps[buf, 0, t * n_ext + HALO : (t + 1) * n_ext, :] + bias[t]
            for a in range(1, QCONV):
                lo = t * n_ext + HALO - a
                conv = conv + ps[buf, a, lo : lo + n_rows, :] * same[a - 1]
            parts.append(conv)
        old = peak[h]
        top = jnp.max(jnp.maximum(parts[0], parts[1]), axis=1, keepdims=True)
        new = jnp.maximum(old, top)
        ws = [jnp.exp(c - new) for c in parts]
        factor = jnp.exp(old - new)
        peak[h] = new
        total[h] = total[h] * factor + jnp.sum(ws[0] + ws[1], axis=1, keepdims=True)
        probs = jnp.concatenate([x.astype(jnp.bfloat16) for x in ws], axis=1)
        upd = jnp.dot(probs, vs[pl.ds(at + 64, 256), :], preferred_element_type=jnp.float32)
        for t in range(GROUP):
            c = slice(t * dh, (t + 1) * dh)
            acc[h, :, c] = acc[h, :, c] * factor + upd[:, c]


def near_kernel(
    info_ref, own_q, own_kv, swap, pa, pb, w, start, same,
    qs, peak, total, acc, ks, vs, score_ok, bias, lhs, ps, sems
):
    side = info_ref[0]
    first_row = info_ref[1]
    rows = own_q.shape[0]
    half = own_q.shape[1]

    def block(n):
        return pl.ds(pl.multiple_of(n * rows, rows), rows)

    copies = [
        (own_q, qs.at[pl.ds(pl.multiple_of(HALO + side * rows, HALO), rows), :]),
        (
            swap.at[0:rows, :],
            qs.at[pl.ds(pl.multiple_of(HALO + (1 - side) * rows, HALO), rows), :],
        ),
        (
            pb.at[0:HALO, :],
            qs.at[pl.ds(pl.multiple_of(side * (2 * rows + HALO), HALO), HALO), :],
        ),
        (
            pa.at[0:HALO, :],
            qs.at[pl.ds(pl.multiple_of((1 - side) * (2 * rows + HALO), HALO), HALO), :],
        ),
    ]
    for src, lo, blk in (
        (own_kv, HALO, 2 + side),
        (swap, rows, 3 - side),
        (pa, HALO, side),
        (pb, HALO, 1 - side),
    ):
        copies.append((src.at[lo : lo + rows, :], ks.at[block(blk), :]))
        copies.append((src.at[lo + rows : lo + 2 * rows, :], vs.at[block(blk), :]))
    started = []
    for n, (src, dst) in enumerate(copies):
        copy = pltpu.make_async_copy(src, dst, sems.at[n])
        copy.start()
        started.append(copy)
    zero = jnp.zeros((rows, half), jnp.bfloat16)
    ks[4 * rows : 5 * rows, :] = zero
    vs[4 * rows : 5 * rows, :] = zero
    peak[...] = jnp.full(peak.shape, FLOOR, jnp.float32)
    total[...] = jnp.zeros(total.shape, jnp.float32)
    acc[...] = jnp.zeros(acc.shape, jnp.float32)
    for copy in started:
        copy.wait()

    def step(n, carry):
        at = pl.multiple_of((1 - n) * 2 * rows, 2 * rows)
        one_window(
            at, first_row - 2 * rows + at, first_row, qs, ks, vs, w, start, same,
            (score_ok, bias), lhs, ps, peak, total, acc,
        )
        return carry

    lax.fori_loop(0, 2, step, 0)


def mid_kernel(
    info_ref, pa, pb, fa, fb, w, start, same, qs, peak_in, total_in, acc_in,
    peak, total, acc, ks, vs, score_ok, bias, lhs, ps, sems
):
    side = info_ref[0]
    first_row = info_ref[1]
    rows = ks.shape[0] // 4

    def block(n):
        return pl.ds(pl.multiple_of(n * rows, rows), rows)

    copies = []
    for src, blk in ((fa, side), (fb, 1 - side), (pa, 2 + side), (pb, 3 - side)):
        copies.append((src.at[HALO : HALO + rows, :], ks.at[block(blk), :]))
        copies.append((src.at[HALO + rows : HALO + 2 * rows, :], vs.at[block(blk), :]))
    copy_all(copies, sems)
    one_window(
        0, first_row - 4 * rows, first_row, qs, ks, vs, w, start, same,
        (score_ok, bias), lhs, ps, peak, total, acc,
    )


def far_kernel(
    info_ref, mix_ref, gain_ref, fa, fb, e0, e1, w, start, same, qs, peak_in, total_in, acc_in,
    mine_ref, theirs_ref, peak, total, acc, ks, vs, score_ok, bias, lhs, ps, normed, sems
):
    side = info_ref[0]
    first_row = info_ref[1]
    rows, half = mine_ref.shape
    n_rows = 2 * rows
    dh = half // GROUP

    def block(n):
        return pl.ds(pl.multiple_of(n * rows, rows), rows)

    copies = []
    for src, blk in ((e0, 1 + 3 * side), (e1, 4 - 3 * side), (fa, 2 + side), (fb, 3 - side)):
        copies.append((src.at[HALO : HALO + rows, :], ks.at[block(blk), :]))
        copies.append((src.at[HALO + rows : HALO + 2 * rows, :], vs.at[block(blk), :]))
    zero = jnp.zeros((rows, half), jnp.bfloat16)
    ks[0:rows, :] = zero
    vs[0:rows, :] = zero
    copy_all(copies, sems)
    one_window(
        0, first_row - 6 * rows, first_row, qs, ks, vs, w, start, same,
        (score_ok, bias), lhs, ps, peak, total, acc,
    )
    base = side * GROUP
    for h in range(GROUP):
        cols = slice(h * dh, (h + 1) * dh)
        out = jnp.zeros((n_rows, dh), jnp.float32)
        for p in range(GROUP):
            out = out + mix_ref[(base + h) * GROUP + p] * (acc[p, :, cols] / total[p])
        mean_sq = jnp.mean(out * out, axis=1, keepdims=True)
        gain = gain_ref[:, pl.ds(pl.multiple_of((base + h) * dh, dh), dh)]
        normed[:, cols] = (out * lax.rsqrt(mean_sq + 1e-06) * gain).astype(jnp.bfloat16)
    mine_ref[...] = normed[block(side), :]
    theirs_ref[...] = normed[block(1 - side), :]


def own_part_kernel(info_ref, x_ref, w_ref, out_ref):
    out_ref[0] = jnp.dot(x_ref[...], w_ref[...], preferred_element_type=jnp.float32)


def add_part_kernel(info_ref, x_ref, w_ref, part_ref, out_ref):
    out = jnp.dot(x_ref[...], w_ref[...], preferred_element_type=jnp.float32)
    out_ref[0] = (out + part_ref[0]).astype(jnp.bfloat16)


def from_behind(block, axis, distance):
    devices = range(lax.axis_size(axis))
    route = [(i - distance, i) for i in devices if i - distance in devices]
    return lax.ppermute(block, axis, route)


def conv_block(scores, theta_part, row_pos, row_start, col_pos, out_cols):
    rim_rows = QCONV - 1
    count_rows = row_pos.shape[0]
    conv_sum = jnp.zeros((scores.shape[0], count_rows, out_cols), jnp.float32)
    above_start = col_pos[None, :] >= row_start[:, None]
    for offset_q in range(QCONV):
        allowed = above_start & (col_pos[None, :] <= row_pos[:, None] - offset_q)
        taken_rows = jnp.where(
            allowed[None],
            scores[:, rim_rows - offset_q : rim_rows - offset_q + count_rows, :],
            jnp.float32(0.0),
        )
        for offset_k in range(KCONV):
            conv_sum = (
                conv_sum
                + theta_part[:, offset_q, KCONV - 1 - offset_k][:, None, None]
                * taken_rows[:, :, offset_k : offset_k + out_cols]
            )
    return conv_sum


def general_plan(queries, keys, values, theta, mix, gain, out_weight, turn_lengths):
    tile_rows = queries.shape[0]
    feature_cols = queries.shape[1]
    local_heads = theta.shape[0]
    head_size = feature_cols // local_heads
    groups = local_heads // GROUP
    group_cols = GROUP * head_size
    rim_rows = QCONV - 1
    key_reach = (KCONV - 1) // 2
    tile_index = lax.axis_index("pb")
    first_row = tile_index * tile_rows
    starts = jnp.cumsum(turn_lengths) - turn_lengths
    row_pos = first_row + jnp.arange(tile_rows, dtype=jnp.int32)
    row_start = jnp.max(jnp.where(starts[None, :] <= row_pos[:, None], starts[None, :], 0), axis=1)
    earlier = from_behind(queries[tile_rows - rim_rows :], "pb", 1)
    query_ext = jnp.concatenate([earlier, queries], 0).reshape(
        tile_rows + rim_rows, local_heads, head_size
    )
    kv_pair = jnp.stack([keys, values], 0)
    window = kv_pair[None]
    while window.shape[0] < MAXBACK + 1:
        have_count = window.shape[0]
        take_count = min(have_count, MAXBACK + 1 - have_count)
        moved_runs = from_behind(window[have_count - take_count :], "pb", have_count)
        window = jnp.concatenate([moved_runs, window], 0)
    key_span = (MAXBACK + 1) * tile_rows
    key_win = window[:, 0].reshape(key_span, feature_cols)
    val_win = window[:, 1].reshape(key_span, feature_cols)
    key_pad = jnp.pad(key_win, ((key_reach, key_reach), (0, 0))).reshape(
        key_span + 2 * key_reach, local_heads, head_size
    )
    key_base = first_row - MAXBACK * tile_rows
    score_scale = 1.0 / math.sqrt(head_size)
    state_carry = (
        jnp.full((local_heads, tile_rows), -1e30, jnp.float32),
        jnp.zeros((local_heads, tile_rows), jnp.float32),
        jnp.zeros((local_heads, tile_rows, group_cols), jnp.float32),
    )
    for block_num in range(MAXBACK + 1):
        block_row_peak, block_row_total, block_accumulated = state_carry
        lower = block_num * tile_rows
        key_slice = key_pad[lower : lower + tile_rows + 2 * key_reach]
        scores = (
            jnp.einsum("rhd,chd->hrc", query_ext, key_slice, preferred_element_type=jnp.float32)
            * score_scale
        )
        col_pos = (
            key_base + lower - key_reach + jnp.arange(tile_rows + 2 * key_reach, dtype=jnp.int32)
        )
        conv_sum = conv_block(scores, theta, row_pos, row_start, col_pos, tile_rows)
        key_pos = key_base + lower + jnp.arange(tile_rows, dtype=jnp.int32)
        keep_mask = (key_pos[None, :] >= row_start[:, None]) & (
            key_pos[None, :] <= row_pos[:, None]
        )
        masked = jnp.where(keep_mask[None], conv_sum, jnp.float32(-1e30))
        new_peak = jnp.maximum(block_row_peak, jnp.max(masked, axis=-1))
        weights = jnp.where(
            keep_mask[None], jnp.exp(conv_sum - new_peak[..., None]), jnp.float32(0.0)
        )
        factor = jnp.exp(block_row_peak - new_peak)
        new_total = block_row_total * factor + jnp.sum(weights, axis=-1)
        prob_bf = weights.astype(jnp.bfloat16).reshape(groups, GROUP, tile_rows, tile_rows)
        val_block = val_win[lower : lower + tile_rows].reshape(tile_rows, groups, group_cols)
        update = jnp.einsum(
            "gpij,jgc->gpic", prob_bf, val_block, preferred_element_type=jnp.float32
        )
        update = update.reshape(local_heads, tile_rows, group_cols)
        state_carry = (new_peak, new_total, block_accumulated * factor[..., None] + update)
    row_peak, row_total, accumulated = state_carry
    normalized = (accumulated / row_total[..., None]).reshape(
        groups, GROUP, tile_rows, GROUP, head_size
    )
    mix_grid = mix.reshape(groups, GROUP, GROUP)
    head_out = jnp.einsum("gkp,gpikd->gikd", mix_grid, normalized)
    head_out = jnp.transpose(head_out, (1, 0, 2, 3)).reshape(tile_rows, local_heads, head_size)
    mean_sq = jnp.mean(head_out * head_out, axis=-1, keepdims=True)
    normed = (
        (head_out * lax.rsqrt(mean_sq + 1e-06) * gain.reshape(local_heads, head_size))
        .reshape(tile_rows, feature_cols)
        .astype(jnp.bfloat16)
    )
    summed = lax.psum_scatter(
        lax.dot_general(
            out_weight, normed, (((0,), (1,)), ((), ())), preferred_element_type=jnp.float32
        ).astype(jnp.bfloat16),
        "ha",
        scatter_dimension=0,
        tiled=True,
    ).astype(jnp.float32)
    return summed.T.astype(jnp.bfloat16)


def paired_plan(queries, keys, values, theta, mix, gain, out_weight, turn_lengths):
    rows, feats = queries.shape
    half = feats // 2
    heads = theta.shape[0]
    dh = feats // heads
    n_pb = lax.axis_size("pb")
    n_ha = lax.axis_size("ha")
    me = lax.axis_index("pb")
    ha = lax.axis_index("ha")
    side = me % 2
    core = ha % 2
    other = n_ha - 2 - (ha - core)
    own_pair = ha - core
    info = jnp.stack(
        [side, (me - side) * rows, other + 1 - core, other + core, own_pair + 1 - core, ha]
    ).astype(jnp.int32)
    vm = pl.BlockSpec(memory_space=pltpu.VMEM)
    sm = pl.BlockSpec(memory_space=pltpu.SMEM)
    anywhere = pl.BlockSpec(memory_space=pl.ANY)
    bf = jnp.bfloat16
    kv_rows = 2 * rows + HALO
    n_rows = 2 * rows
    n_ext = n_rows + HALO
    shape = jax.ShapeDtypeStruct
    params = pltpu.CompilerParams(vmem_limit_bytes=28 * 1024 * 1024)

    own_q, own_kv, oth_all, oth_kv = pl.pallas_call(
        split_kernel,
        out_shape=(
            shape((rows, half), bf),
            shape((kv_rows, half), bf),
            shape((3 * rows, half), bf),
            shape((kv_rows, half), bf),
        ),
        in_specs=[sm, vm, vm, vm],
        out_specs=(vm, vm, vm, vm),
    )(info, queries, keys, values)

    pairs = range(n_pb)
    up = [(i, i + 2) for i in pairs if i + 2 < n_pb]
    cross = [(i, (i ^ 1) + 2) for i in pairs if (i ^ 1) + 2 < n_pb]
    swap_route = [(i, i ^ 1) for i in pairs]
    far = [(i, i + MAXBACK) for i in pairs if i % 2 == 1 and i + MAXBACK < n_pb]
    up_odd = [(i, i + 2) for i in pairs if i % 2 == 1 and i + 2 < n_pb]

    pa = move(own_kv, "pb", up)
    pbk = move(oth_kv, "pb", cross)
    swap = move(oth_all, "pb", swap_route)
    e0 = move(oth_kv, "pb", far)

    n_pair = GROUP * QCONV // 2
    w, start, same = pl.pallas_call(
        functools.partial(prep_kernel, scale=1.0 / math.sqrt(dh)),
        out_shape=(
            shape((n_pair, 256, 256), bf),
            shape((n_ext, 128), jnp.int32),
            shape((QCONV - 1, n_rows, 128), jnp.float32),
        ),
        in_specs=[sm, sm, sm],
        out_specs=(vm, vm, vm),
        cost_estimate=pl.CostEstimate(
            flops=20_000_000, bytes_accessed=2_400_000, transcendentals=0
        ),
    )(info, turn_lengths, theta.reshape(-1))
    pa, w = lax.optimization_barrier((pa, w))
    fa = move(pa, "pb", up)
    fb = move(pbk, "pb", up)
    e1 = move(fa, "pb", up_odd)

    state = (
        shape((GROUP, n_rows, 128), jnp.float32),
        shape((GROUP, n_rows, 128), jnp.float32),
        shape((GROUP, n_rows, half), jnp.float32),
    )
    work = [
        pltpu.VMEM((3, n_ext, 128), jnp.float32),
        pltpu.VMEM((2, n_rows, 128), jnp.float32),
        pltpu.VMEM((2, 2 * n_ext, 256), bf),
        pltpu.VMEM((2, QCONV, 2 * n_ext, 128), jnp.float32),
    ]

    def cost(n):
        return pl.CostEstimate(
            flops=n * 1_500_000_000, bytes_accessed=n * 6_000_000, transcendentals=n * 300_000
        )

    qs, peak, total, acc = pl.pallas_call(
        near_kernel,
        out_shape=(shape((n_ext + HALO, half), bf),) + state,
        in_specs=[sm] + [anywhere] * 5 + [vm] * 3,
        out_specs=(vm,) * 4,
        scratch_shapes=[pltpu.VMEM((5 * rows, half), bf)] * 2
        + work
        + [pltpu.SemaphoreType.DMA((12,))],
        compiler_params=params,
        cost_estimate=cost(2),
    )(info, own_q, own_kv, swap, pa, pbk, w, start, same)
    peak, total, acc = pl.pallas_call(
        mid_kernel,
        out_shape=state,
        in_specs=[sm] + [anywhere] * 4 + [vm] * 7,
        out_specs=(vm,) * 3,
        input_output_aliases={9: 0, 10: 1, 11: 2},
        scratch_shapes=[pltpu.VMEM((4 * rows, half), bf)] * 2
        + work
        + [pltpu.SemaphoreType.DMA((8,))],
        compiler_params=params,
        cost_estimate=cost(1),
    )(info, pa, pbk, fa, fb, w, start, same, qs, peak, total, acc)
    mine, theirs, _, _, _ = pl.pallas_call(
        far_kernel,
        out_shape=(shape((rows, half), bf), shape((rows, half), bf)) + state,
        in_specs=[sm, sm, vm] + [anywhere] * 4 + [vm] * 7,
        out_specs=(vm,) * 5,
        input_output_aliases={11: 2, 12: 3, 13: 4},
        scratch_shapes=[pltpu.VMEM((5 * rows, half), bf)] * 2
        + work
        + [pltpu.VMEM((n_rows, half), bf), pltpu.SemaphoreType.DMA((8,))],
        compiler_params=params,
        cost_estimate=cost(1),
    )(
        info, mix.reshape(-1), gain.reshape(1, -1), fa, fb, e0, e1, w, start, same, qs,
        peak, total, acc,
    )

    got = move(theirs, "pb", swap_route)
    cols = out_weight.shape[1]
    part = cols // n_ha
    part_bytes = half * part * 2
    own_part = pl.pallas_call(
        own_part_kernel,
        out_shape=shape((n_ha, rows, part), jnp.float32),
        grid_spec=pltpu.PrefetchScalarGridSpec(
            num_scalar_prefetch=1,
            grid=(n_ha,),
            in_specs=[
                pl.BlockSpec((rows, half), lambda i, s: (0, 0)),
                pl.BlockSpec((half, part), lambda i, s: (s[0], s[2 + i])),
            ],
            out_specs=pl.BlockSpec((1, rows, part), lambda i, s: (i, 0, 0)),
        ),
        cost_estimate=pl.CostEstimate(
            flops=2 * rows * half * cols, bytes_accessed=6 * part_bytes, transcendentals=0
        ),
    )(info, mine, out_weight)

    def finish(lo):
        return pl.pallas_call(
            add_part_kernel,
            out_shape=shape((2, rows, part), bf),
            grid_spec=pltpu.PrefetchScalarGridSpec(
                num_scalar_prefetch=1,
                grid=(2,),
                in_specs=[
                    pl.BlockSpec((rows, half), lambda i, s: (0, 0)),
                    pl.BlockSpec((half, part), lambda i, s: (1 - s[0], s[2 + lo + i])),
                    pl.BlockSpec((1, rows, part), lambda i, s: (lo + i, 0, 0)),
                ],
                out_specs=pl.BlockSpec((1, rows, part), lambda i, s: (i, 0, 0)),
            ),
            cost_estimate=pl.CostEstimate(
                flops=rows * half * cols, bytes_accessed=4 * part_bytes, transcendentals=0
            ),
        )(info, got, out_weight, own_part)

    def exchange(two):
        take = move(two[0], "ha", [(i, i ^ 1) for i in range(n_ha)])
        return two[1].astype(jnp.float32) + take.astype(jnp.float32)

    away = exchange(finish(0)).astype(bf)
    arrived = move(away, "ha", [(i, i ^ 2) for i in range(n_ha)])
    here = exchange(finish(2))
    return (here + arrived.astype(jnp.float32)).astype(bf)


def per_device(queries, keys, values, theta, mix, gain, out_weight, turn_lengths):
    rows, feats = queries.shape
    heads = theta.shape[0]
    fits = rows == 128 and feats == 128 * heads and heads == 2 * GROUP
    n_pb, n_ha = lax.axis_size("pb"), lax.axis_size("ha")
    fits = fits and n_pb % 2 == 0 and n_ha == 4
    plan = paired_plan if fits else general_plan
    return plan(queries, keys, values, theta, mix, gain, out_weight, turn_lengths)


def solution(mesh):
    return jax.shard_map(
        per_device,
        mesh=mesh,
        in_specs=(
            P("pb", "ha"),
            P("pb", "ha"),
            P("pb", "ha"),
            P("ha", None, None),
            P("ha", None),
            P("ha"),
            P("ha", None),
            P(),
        ),
        out_specs=P("pb", "ha"),
        check_vma=False,
    )
```

```python
import functools
import math

import jax
import jax.numpy as jnp
from jax import lax
from jax.experimental import pallas as pl
from jax.experimental.pallas import tpu as pltpu
from jax.sharding import PartitionSpec as P


GROUP = 4
QCONV = 6
KCONV = 11
MAXBACK = 5
HALO = 16
NEG = -1e30
FLOOR = -5e29


def place():
    me = lax.axis_index("pb")
    side = lax.rem(me, 2)
    return side, me - side


def copy_all(copies, sems):
    started = []
    for n, (src, dst) in enumerate(copies):
        copy = pltpu.make_async_copy(src, dst, sems.at[n])
        copy.start()
        started.append(copy)
    for copy in started:
        copy.wait()


def first_kernel(q_ref, k_ref, v_ref, own_kv, sems):
    side, _ = place()
    rows = q_ref.shape[0]
    half = q_ref.shape[1] // 2
    own = pl.ds(pl.multiple_of(side * half, half), half)
    copy_all(
        [
            (k_ref.at[:, own], own_kv.at[HALO : HALO + rows, :]),
            (v_ref.at[:, own], own_kv.at[HALO + rows : HALO + 2 * rows, :]),
            (q_ref.at[rows - HALO : rows, own], own_kv.at[0:HALO, :]),
        ],
        sems,
    )


def split_kernel(q_ref, k_ref, v_ref, own_q, oth_all, oth_kv, sems):
    side, _ = place()
    rows = q_ref.shape[0]
    half = q_ref.shape[1] // 2
    own = pl.ds(pl.multiple_of(side * half, half), half)
    oth = pl.ds(pl.multiple_of((1 - side) * half, half), half)
    copy_all(
        [
            (k_ref.at[:, oth], oth_kv.at[HALO : HALO + rows, :]),
            (v_ref.at[:, oth], oth_kv.at[HALO + rows : HALO + 2 * rows, :]),
            (q_ref.at[rows - HALO : rows, oth], oth_kv.at[0:HALO, :]),
            (q_ref.at[:, oth], oth_all.at[0:rows, :]),
            (k_ref.at[:, oth], oth_all.at[rows : 2 * rows, :]),
            (v_ref.at[:, oth], oth_all.at[2 * rows : 3 * rows, :]),
            (q_ref.at[:, own], own_q),
        ],
        sems,
    )


def prep_kernel(
    len_ref, theta_ref, mix_ref, gain_ref, out_weight,
    w_ref, start_ref, same_ref, w_own, blend_ref, gain_out, sems, *, scale
):
    reach = (KCONV - 1) // 2
    width = 128
    side_here, first = place()
    copies = load_weights(out_weight, w_own, side_here, sems)
    base = side_here * GROUP
    first_row = first * ((start_ref.shape[0] - HALO) // 2)
    diff = lax.broadcasted_iota(jnp.int32, (width, width), 1) - lax.broadcasted_iota(
        jnp.int32, (width, width), 0
    )

    def body(step, carry):
        h = step // (QCONV // 2)
        q = step % (QCONV // 2)
        for side in range(2):
            lo = jnp.zeros((width, width), jnp.float32)
            hi = jnp.zeros((width, width), jnp.float32)
            tap = 2 * q + side
            for b in range(-reach, reach + 1):
                t = theta_ref[tap, base + h, b + reach] * scale
                lo = jnp.where(diff == b - 64, t, lo)
                hi = jnp.where(diff == b + 64, t, hi)
            w_ref[step, 0:width, side * width : (side + 1) * width] = lo.astype(jnp.bfloat16)
            w_ref[step, width : 2 * width, side * width : (side + 1) * width] = hi.astype(
                jnp.bfloat16
            )
        return carry

    lax.fori_loop(0, GROUP * QCONV // 2, body, 0)
    for p in range(GROUP):
        for h in range(GROUP):
            n = p * GROUP + h
            blend_ref[n : n + 1, :] = jnp.full((1, width), mix_ref[p, base + h], jnp.float32)
    half = gain_out.shape[1]
    gain_out[...] = gain_ref[:, pl.ds(pl.multiple_of(side_here * half, half), half)]
    shape = start_ref.shape
    row = first_row - HALO + lax.broadcasted_iota(jnp.int32, shape, 0)
    start = jnp.zeros(shape, jnp.int32)
    begin = jnp.int32(0)
    for n in range(len_ref.shape[0]):
        start = jnp.where(row >= begin, begin, start)
        begin = begin + len_ref[n]
    start_ref[...] = start
    for a in range(1, QCONV):
        same_ref[a - 1] = (row[HALO:] - a >= start[HALO:]).astype(jnp.float32)
    for copy in copies:
        copy.wait()


def window_masks(col0, first_row, row0, n_rows, start, score_ok, bias):
    n_ext = n_rows + HALO
    lane = lax.broadcasted_iota(jnp.int32, (1, 128), 1)
    start_ext = start[pl.ds(row0, n_ext), :]
    row_ext = first_row + row0 - HALO + lax.broadcasted_iota(jnp.int32, (n_ext, 128), 0)
    for t in range(3):
        col = col0 + t * 128 + lane
        ok = (col >= start_ext) & (col <= row_ext)
        score_ok[t] = jnp.where(ok, 1.0, 0.0)
    for t in range(2):
        col = col0 + 64 + t * 128 + lane
        ok = (col >= start_ext[HALO:]) & (col <= row_ext[HALO:])
        bias[t] = jnp.where(ok, 0.0, NEG)


def reaches(start, row0, col0):
    return jnp.min(start[row0 + HALO : row0 + HALO + 8, :]) < col0 + 64 + 256


def one_window(at, row0, n_rows, qs, ks, vs, w, same, work, state, result):
    score_ok, bias, lhs, ps, probs, factors = work
    peak, total, acc = state
    peak_out, total_out, acc_out = result
    n_ext = n_rows + HALO
    dh = 128
    n_q = QCONV // 2
    step = 64

    def scores(h):
        cols = slice(h * dh, (h + 1) * dh)
        buf = h % 2
        s = lax.dot_general(
            qs[pl.ds(row0, n_ext), cols],
            ks[pl.ds(at, 384), cols],
            (((1,), (1,)), ((), ())),
            preferred_element_type=jnp.float32,
        )
        for t in range(3):
            piece = (s[:, t * 128 : (t + 1) * 128] * score_ok[t]).astype(jnp.bfloat16)
            if t < 2:
                lhs[buf, 0:n_ext, t * 128 : (t + 1) * 128] = piece
            if t > 0:
                lhs[buf, n_ext : 2 * n_ext, (t - 1) * 128 : t * 128] = piece

    def taps(h, q):
        buf = h % 2
        pair = jnp.dot(lhs[buf], w[h * n_q + q], preferred_element_type=jnp.float32)
        ps[buf, 2 * q] = pair[:, 0:128]
        ps[buf, 2 * q + 1] = pair[:, 128:256]

    def weigh(h, r):
        buf = h % 2
        rows = pl.ds(row0 + r, step)
        keep = [same[a - 1, rows, :] for a in range(1, QCONV)]
        parts = []
        for t in range(2):
            base = t * n_ext + HALO + r
            conv = ps[buf, 0, base : base + step, :] + bias[t, r : r + step, :]
            for a in range(1, QCONV):
                conv = conv + ps[buf, a, base - a : base - a + step, :] * keep[a - 1]
            parts.append(conv)
        old = peak[h, rows, :]
        top = jnp.max(jnp.maximum(parts[0], parts[1]), axis=1, keepdims=True)
        new = jnp.maximum(old, top)
        ws = [jnp.exp(c - new) for c in parts]
        factor = jnp.exp(old - new)
        if peak_out is not None:
            peak_out[h, rows, :] = new
        out_rows = rows if peak_out is not None else pl.ds(r, step)
        total_out[h, out_rows, :] = total[h, rows, :] * factor + jnp.sum(
            ws[0] + ws[1], axis=1, keepdims=True
        )
        factors[buf, r : r + step, :] = factor
        for t in range(2):
            probs[buf, r : r + step, t * 128 : (t + 1) * 128] = ws[t].astype(jnp.bfloat16)

    def gather(h):
        buf = h % 2
        out_rows = pl.ds(row0, n_rows) if peak_out is not None else pl.ds(0, n_rows)
        upd = jnp.dot(
            probs[buf], vs[pl.ds(at + 64, 256), :], preferred_element_type=jnp.float32
        )
        factor = factors[buf]
        for t in range(GROUP):
            c = slice(t * dh, (t + 1) * dh)
            acc_out[h, out_rows, c] = acc[h, pl.ds(row0, n_rows), c] * factor + upd[:, c]

    chunks = list(range(0, n_rows, step))
    scores(0)
    for q in range(n_q):
        taps(0, q)
    for h in range(GROUP):
        more = h + 1 < GROUP
        if more:
            scores(h + 1)
        for n in range(max(len(chunks), n_q)):
            if n < len(chunks):
                weigh(h, chunks[n])
            if more and n < n_q:
                taps(h + 1, n)
        gather(h)


def put(src, lo, ks, vs, blk):
    rows = (src.shape[0] - lo) // 2
    at = pl.ds(pl.multiple_of(blk * rows, rows), rows)
    ks[at, :] = src[lo : lo + rows, :]
    vs[at, :] = src[lo + rows : lo + 2 * rows, :]


def load_weights(out_weight, dst, who, sems):
    half, part = dst.shape[1:]
    ha = lax.axis_index("ha")
    core = lax.rem(ha, 2)
    pair = ha - core
    away = 2 - pair
    order = (away + 1 - core, away + core, pair + 1 - core, ha)
    copies = []
    for n in range(dst.shape[0]):
        rows = pl.ds(pl.multiple_of(who * half, half), half)
        cols = pl.ds(pl.multiple_of(order[n] * part, part), part)
        copy = pltpu.make_async_copy(out_weight.at[rows, cols], dst.at[n], sems.at[n])
        copy.start()
        copies.append(copy)
    return copies


def own_kernel(
    own_q, own_kv, swap, out_weight, w, start, same,
    qs, ks, vs, peak, total, acc, w_oth, e_src, score_ok, bias, lhs, ps, probs, factors, sems
):
    rows, half = own_q.shape
    side, first = place()
    first_row = first * rows
    copies = load_weights(out_weight, w_oth, 1 - side, sems)
    qs[pl.ds(pl.multiple_of(HALO + side * rows, HALO), rows), :] = own_q[...]
    qs[pl.ds(pl.multiple_of(HALO + (1 - side) * rows, HALO), rows), :] = swap[0:rows, :]

    qs[0:HALO, :] = jnp.zeros((HALO, half), jnp.bfloat16)

    @pl.when(side == 0)
    def _():
        e_src[...] = swap[rows : 3 * rows, :]

    @pl.when(side == 1)
    def _():
        e_src[...] = own_kv[HALO : HALO + 2 * rows, :]

    zero = jnp.zeros((rows, half), jnp.bfloat16)
    for blk in (0, 1, 8):
        ks[blk * rows : (blk + 1) * rows, :] = zero
        vs[blk * rows : (blk + 1) * rows, :] = zero
    put(own_kv, HALO, ks, vs, 6 + side)
    put(swap, rows, ks, vs, 7 - side)
    peak[...] = jnp.full(peak.shape, FLOOR, jnp.float32)
    total[...] = jnp.zeros(total.shape, jnp.float32)
    acc[...] = jnp.zeros(acc.shape, jnp.float32)
    state = (peak, total, acc)
    window_masks(first_row, first_row, 0, 2 * rows, start, score_ok, bias)
    one_window(
        6 * rows, 0, 2 * rows, qs, ks, vs, w, same,
        (score_ok, bias, lhs, ps, probs, factors), state, state,
    )
    for copy in copies:
        copy.wait()


def next_kernel(
    pa, pb, w, start, same, qs_in, ks_in, vs_in, peak_in, total_in, acc_in,
    qs, ks, vs, peak, total, acc, score_ok, bias, lhs, ps, probs, factors
):
    rows = (qs.shape[0] - HALO) // 2
    side, first = place()
    first_row = first * rows
    put(pa, HALO, ks, vs, 4 + side)
    put(pb, HALO, ks, vs, 5 - side)

    @pl.when(side == 0)
    def _():
        qs[0:HALO, :] = pb[0:HALO, :]

    @pl.when(side == 1)
    def _():
        qs[0:HALO, :] = pa[0:HALO, :]

    state = (peak, total, acc)
    window_masks(first_row - 2 * rows, first_row, 0, 2 * rows, start, score_ok, bias)
    one_window(
        4 * rows, 0, 2 * rows, qs, ks, vs, w, same,
        (score_ok, bias, lhs, ps, probs, factors), state, state,
    )


def mid_kernel(
    fa, fb, w, start, same, qs, ks_in, vs_in, peak_in, total_in, acc_in,
    ks, vs, peak, total, acc, score_ok, bias, lhs, ps, probs, factors
):
    rows = (qs.shape[0] - HALO) // 2
    side, first = place()
    first_row = first * rows
    put(fa, HALO, ks, vs, 2 + side)
    put(fb, HALO, ks, vs, 3 - side)
    state = (peak, total, acc)

    @pl.when(reaches(start, 0, first_row - 4 * rows))
    def _():
        window_masks(first_row - 4 * rows, first_row, 0, 2 * rows, start, score_ok, bias)
        one_window(
            2 * rows, 0, 2 * rows, qs, ks, vs, w, same,
            (score_ok, bias, lhs, ps, probs, factors), state, state,
        )


def finish_rows(
    mix_ref, gain_ref, row0, out_ref, ks, vs, w, start, same, qs, peak, total, acc,
    score_ok, bias, lhs, ps, probs, factors, total_end, acc_end
):
    rows, half = out_ref.shape
    _, first = place()
    first_row = first * rows
    dh = half // GROUP
    needed = reaches(start, row0, first_row - 6 * rows)

    @pl.when(needed)
    def _():
        window_masks(first_row - 6 * rows, first_row, row0, rows, start, score_ok, bias)
        one_window(
            0, row0, rows, qs, ks, vs, w, same, (score_ok, bias, lhs, ps, probs, factors),
            (peak, total, acc), (None, total_end, acc_end),
        )

    @pl.when(jnp.logical_not(needed))
    def _():
        total_end[...] = total[:, row0 : row0 + rows, :]
        acc_end[...] = acc[:, row0 : row0 + rows, :]

    inverse = [1.0 / total_end[p] for p in range(GROUP)]
    for h in range(GROUP):
        cols = slice(h * dh, (h + 1) * dh)
        out = jnp.zeros((rows, dh), jnp.float32)
        for p in range(GROUP):
            n = p * GROUP + h
            out = out + mix_ref[n : n + 1, :] * (acc_end[p, :, cols] * inverse[p])
        mean_sq = jnp.mean(out * out, axis=1, keepdims=True)
        out_ref[:, cols] = (out * lax.rsqrt(mean_sq + 1e-06) * gain_ref[:, cols]).astype(
            jnp.bfloat16
        )


def odd_kernel(
    mix_ref, gain_ref, w, start, same, qs, ks, vs, peak, total, acc,
    out_ref, score_ok, bias, lhs, ps, probs, factors, total_end, acc_end
):
    finish_rows(
        mix_ref, gain_ref, out_ref.shape[0], out_ref, ks, vs, w, start, same, qs, peak, total,
        acc, score_ok, bias, lhs, ps, probs, factors, total_end, acc_end,
    )


def even_kernel(
    mix_ref, gain_ref, odd_ref, last, w, start, same, qs, ks_in, vs_in, peak, total, acc,
    mine_ref, theirs_ref, ks, vs,
    score_ok, bias, lhs, ps, probs, factors, total_end, acc_end, even_ref
):
    side, _ = place()
    put(last, 0, ks, vs, 1)
    finish_rows(
        mix_ref, gain_ref, 0, even_ref, ks, vs, w, start, same, qs, peak, total,
        acc, score_ok, bias, lhs, ps, probs, factors, total_end, acc_end,
    )

    @pl.when(side == 0)
    def _():
        mine_ref[...] = even_ref[...]
        theirs_ref[...] = odd_ref[...]

    @pl.when(side == 1)
    def _():
        mine_ref[...] = odd_ref[...]
        theirs_ref[...] = even_ref[...]


def own_part_kernel(x_ref, w_ref, out_ref):
    for n in range(w_ref.shape[0]):
        out_ref[n] = jnp.dot(x_ref[...], w_ref[n], preferred_element_type=jnp.float32)


def add_part_kernel(x_ref, w_ref, part_ref, give_ref, keep_ref, *, lo):
    for n, out_ref in enumerate((give_ref, keep_ref)):
        out = jnp.dot(x_ref[...], w_ref[lo + n], preferred_element_type=jnp.float32)
        out_ref[...] = (out + part_ref[lo + n]).astype(jnp.bfloat16)


def from_behind(block, axis, distance):
    devices = range(lax.axis_size(axis))
    route = [(i - distance, i) for i in devices if i - distance in devices]
    return lax.ppermute(block, axis, route)


def conv_block(scores, theta_part, row_pos, row_start, col_pos, out_cols):
    rim_rows = QCONV - 1
    count_rows = row_pos.shape[0]
    conv_sum = jnp.zeros((scores.shape[0], count_rows, out_cols), jnp.float32)
    above_start = col_pos[None, :] >= row_start[:, None]
    for offset_q in range(QCONV):
        allowed = above_start & (col_pos[None, :] <= row_pos[:, None] - offset_q)
        taken_rows = jnp.where(
            allowed[None],
            scores[:, rim_rows - offset_q : rim_rows - offset_q + count_rows, :],
            jnp.float32(0.0),
        )
        for offset_k in range(KCONV):
            conv_sum = (
                conv_sum
                + theta_part[:, offset_q, KCONV - 1 - offset_k][:, None, None]
                * taken_rows[:, :, offset_k : offset_k + out_cols]
            )
    return conv_sum


def general_plan(queries, keys, values, theta, mix, gain, out_weight, turn_lengths):
    tile_rows = queries.shape[0]
    feature_cols = queries.shape[1]
    local_heads = theta.shape[0]
    head_size = feature_cols // local_heads
    groups = local_heads // GROUP
    group_cols = GROUP * head_size
    rim_rows = QCONV - 1
    key_reach = (KCONV - 1) // 2
    tile_index = lax.axis_index("pb")
    first_row = tile_index * tile_rows
    starts = jnp.cumsum(turn_lengths) - turn_lengths
    row_pos = first_row + jnp.arange(tile_rows, dtype=jnp.int32)
    row_start = jnp.max(jnp.where(starts[None, :] <= row_pos[:, None], starts[None, :], 0), axis=1)
    earlier = from_behind(queries[tile_rows - rim_rows :], "pb", 1)
    query_ext = jnp.concatenate([earlier, queries], 0).reshape(
        tile_rows + rim_rows, local_heads, head_size
    )
    kv_pair = jnp.stack([keys, values], 0)
    window = kv_pair[None]
    while window.shape[0] < MAXBACK + 1:
        have_count = window.shape[0]
        take_count = min(have_count, MAXBACK + 1 - have_count)
        moved_runs = from_behind(window[have_count - take_count :], "pb", have_count)
        window = jnp.concatenate([moved_runs, window], 0)
    key_span = (MAXBACK + 1) * tile_rows
    key_win = window[:, 0].reshape(key_span, feature_cols)
    val_win = window[:, 1].reshape(key_span, feature_cols)
    key_pad = jnp.pad(key_win, ((key_reach, key_reach), (0, 0))).reshape(
        key_span + 2 * key_reach, local_heads, head_size
    )
    key_base = first_row - MAXBACK * tile_rows
    score_scale = 1.0 / math.sqrt(head_size)
    state_carry = (
        jnp.full((local_heads, tile_rows), -1e30, jnp.float32),
        jnp.zeros((local_heads, tile_rows), jnp.float32),
        jnp.zeros((local_heads, tile_rows, group_cols), jnp.float32),
    )
    for block_num in range(MAXBACK + 1):
        block_row_peak, block_row_total, block_accumulated = state_carry
        lower = block_num * tile_rows
        key_slice = key_pad[lower : lower + tile_rows + 2 * key_reach]
        scores = (
            jnp.einsum("rhd,chd->hrc", query_ext, key_slice, preferred_element_type=jnp.float32)
            * score_scale
        )
        col_pos = (
            key_base + lower - key_reach + jnp.arange(tile_rows + 2 * key_reach, dtype=jnp.int32)
        )
        conv_sum = conv_block(scores, theta, row_pos, row_start, col_pos, tile_rows)
        key_pos = key_base + lower + jnp.arange(tile_rows, dtype=jnp.int32)
        keep_mask = (key_pos[None, :] >= row_start[:, None]) & (
            key_pos[None, :] <= row_pos[:, None]
        )
        masked = jnp.where(keep_mask[None], conv_sum, jnp.float32(-1e30))
        new_peak = jnp.maximum(block_row_peak, jnp.max(masked, axis=-1))
        weights = jnp.where(
            keep_mask[None], jnp.exp(conv_sum - new_peak[..., None]), jnp.float32(0.0)
        )
        factor = jnp.exp(block_row_peak - new_peak)
        new_total = block_row_total * factor + jnp.sum(weights, axis=-1)
        prob_bf = weights.astype(jnp.bfloat16).reshape(groups, GROUP, tile_rows, tile_rows)
        val_block = val_win[lower : lower + tile_rows].reshape(tile_rows, groups, group_cols)
        update = jnp.einsum(
            "gpij,jgc->gpic", prob_bf, val_block, preferred_element_type=jnp.float32
        )
        update = update.reshape(local_heads, tile_rows, group_cols)
        state_carry = (new_peak, new_total, block_accumulated * factor[..., None] + update)
    _, row_total, accumulated = state_carry
    normalized = (accumulated / row_total[..., None]).reshape(
        groups, GROUP, tile_rows, GROUP, head_size
    )
    mix_grid = mix.reshape(groups, GROUP, GROUP)
    head_out = jnp.einsum("gkp,gpikd->gikd", mix_grid, normalized)
    head_out = jnp.transpose(head_out, (1, 0, 2, 3)).reshape(tile_rows, local_heads, head_size)
    mean_sq = jnp.mean(head_out * head_out, axis=-1, keepdims=True)
    normed = (
        (head_out * lax.rsqrt(mean_sq + 1e-06) * gain.reshape(local_heads, head_size))
        .reshape(tile_rows, feature_cols)
        .astype(jnp.bfloat16)
    )
    summed = lax.psum_scatter(
        lax.dot_general(
            out_weight, normed, (((0,), (1,)), ((), ())), preferred_element_type=jnp.float32
        ).astype(jnp.bfloat16),
        "ha",
        scatter_dimension=0,
        tiled=True,
    ).astype(jnp.float32)
    return summed.T.astype(jnp.bfloat16)


def paired_plan(queries, keys, values, theta, mix, gain, out_weight, turn_lengths):
    rows, feats = queries.shape
    half = feats // 2
    heads = theta.shape[0]
    dh = feats // heads
    n_pb = lax.axis_size("pb")
    n_ha = lax.axis_size("ha")
    vm = pl.BlockSpec(memory_space=pltpu.VMEM)
    sm = pl.BlockSpec(memory_space=pltpu.SMEM)
    hbm = pl.BlockSpec(memory_space=pltpu.HBM)
    stay = functools.partial(pltpu.with_memory_space_constraint, memory_space=pltpu.HBM)
    small = pltpu.CompilerParams(vmem_limit_bytes=8 * 1024 * 1024)
    bf = jnp.bfloat16
    f32 = jnp.float32
    kv_rows = 2 * rows + HALO
    n_rows = 2 * rows
    n_ext = n_rows + HALO
    on_chip = pltpu.VMEM
    params = pltpu.CompilerParams(vmem_limit_bytes=24 * 1024 * 1024)

    inputs = (stay(queries), stay(keys), stay(values))
    own_kv = pl.pallas_call(
        first_kernel,
        out_shape=on_chip((kv_rows, half), bf),
        in_specs=[hbm] * 3,
        out_specs=vm,
        scratch_shapes=[pltpu.SemaphoreType.DMA((3,))],
        compiler_params=small,
    )(*inputs)
    own_q, oth_all, oth_kv = pl.pallas_call(
        split_kernel,
        out_shape=(
            on_chip((rows, half), bf),
            on_chip((3 * rows, half), bf),
            on_chip((kv_rows, half), bf),
        ),
        in_specs=[hbm] * 3,
        out_specs=(vm, vm, vm),
        scratch_shapes=[pltpu.SemaphoreType.DMA((7,))],
        compiler_params=small,
    )(*inputs)

    pairs = range(n_pb)
    up = [(i, i + 2) for i in pairs if i + 2 < n_pb]
    cross = [(i, (i ^ 1) + 2) for i in pairs if (i ^ 1) + 2 < n_pb]
    swap_route = [(i, i ^ 1) for i in pairs]
    far = [(i, i + MAXBACK + 1) for i in pairs if i + MAXBACK + 1 < n_pb]

    pa = lax.ppermute(own_kv, "pb", up)
    pbk = lax.ppermute(oth_kv, "pb", cross)
    swap = lax.ppermute(oth_all, "pb", swap_route)

    n_pair = GROUP * QCONV // 2
    cols = out_weight.shape[1]
    part = cols // n_ha
    weights = on_chip((n_ha, half, part), bf)
    heavy = stay(out_weight)
    prep_params = pltpu.CompilerParams(vmem_limit_bytes=16 * 1024 * 1024)
    w, start, same, w_own, blend, gain_own = pl.pallas_call(
        functools.partial(prep_kernel, scale=1.0 / math.sqrt(dh)),
        out_shape=(
            on_chip((n_pair, 256, 256), bf),
            on_chip((n_ext, 128), jnp.int32),
            on_chip((QCONV - 1, n_rows, 128), f32),
            weights,
            on_chip((GROUP * GROUP, 128), f32),
            on_chip((1, half), f32),
        ),
        in_specs=[sm, sm, sm, vm, hbm],
        out_specs=(vm,) * 6,
        scratch_shapes=[pltpu.SemaphoreType.DMA((n_ha,))],
        compiler_params=prep_params,
        cost_estimate=pl.CostEstimate(
            flops=20_000_000, bytes_accessed=2_400_000, transcendentals=0
        ),
    )(stay(turn_lengths), stay(theta.transpose(1, 0, 2)), stay(mix.T), stay(gain.reshape(1, -1)), heavy)
    pa, w = lax.optimization_barrier((pa, w))
    fa = lax.ppermute(pa, "pb", up)
    fb = lax.ppermute(pbk, "pb", up)

    def state(make):
        return (
            make((GROUP, n_rows, 128), f32),
            make((GROUP, n_rows, 128), f32),
            make((GROUP, n_rows, half), f32),
        )

    def work(count):
        ext = count + HALO
        return [
            pltpu.VMEM((3, ext, 128), f32),
            pltpu.VMEM((2, count, 128), f32),
            pltpu.VMEM((2, 2 * ext, 256), bf),
            pltpu.VMEM((2, QCONV, 2 * ext, 128), f32),
            pltpu.VMEM((2, count, 256), bf),
            pltpu.VMEM((2, count, 128), f32),
        ]

    def cost(n):
        return pl.CostEstimate(
            flops=int(n * 1_500_000_000),
            bytes_accessed=int(n * 6_000_000),
            transcendentals=int(n * 300_000),
        )

    span = on_chip((9 * rows, half), bf)
    qs, ks, vs, peak, total, acc, w_oth, e_src = pl.pallas_call(
        own_kernel,
        out_shape=(on_chip((n_ext, half), bf), span, span)
        + state(on_chip)
        + (weights, on_chip((2 * rows, half), bf)),
        in_specs=[vm] * 3 + [hbm] + [vm] * 3,
        out_specs=(vm,) * 8,
        scratch_shapes=work(n_rows) + [pltpu.SemaphoreType.DMA((n_ha,))],
        compiler_params=params,
        cost_estimate=cost(1),
    )(own_q, own_kv, swap, heavy, w, start, same)
    last = lax.ppermute(e_src, "pb", far)
    qs, ks, vs, peak, total, acc = pl.pallas_call(
        next_kernel,
        out_shape=(on_chip((n_ext, half), bf), span, span) + state(on_chip),
        in_specs=[vm] * 11,
        out_specs=(vm,) * 6,
        input_output_aliases={5: 0, 6: 1, 7: 2, 8: 3, 9: 4, 10: 5},
        scratch_shapes=work(n_rows),
        compiler_params=params,
        cost_estimate=cost(1),
    )(pa, pbk, w, start, same, qs, ks, vs, peak, total, acc)
    ks, vs, peak, total, acc = pl.pallas_call(
        mid_kernel,
        out_shape=(span, span) + state(on_chip),
        in_specs=[vm] * 11,
        out_specs=(vm,) * 5,
        input_output_aliases={6: 0, 7: 1, 8: 2, 9: 3, 10: 4},
        scratch_shapes=work(n_rows),
        compiler_params=params,
        cost_estimate=cost(1),
    )(fa, fb, w, start, same, qs, ks, vs, peak, total, acc)
    ends = [pltpu.VMEM((GROUP, rows, 128), f32), pltpu.VMEM((GROUP, rows, half), f32)]
    odd = pl.pallas_call(
        odd_kernel,
        out_shape=on_chip((rows, half), bf),
        in_specs=[vm] * 11,
        out_specs=vm,
        scratch_shapes=work(rows) + ends,
        compiler_params=params,
        cost_estimate=cost(0.5),
    )(blend, gain_own, w, start, same, qs, ks, vs, peak, total, acc)
    last, odd = lax.optimization_barrier((last, odd))
    mine, theirs, _, _ = pl.pallas_call(
        even_kernel,
        out_shape=(on_chip((rows, half), bf),) * 2 + (span, span),
        in_specs=[vm] * 13,
        out_specs=(vm,) * 4,
        input_output_aliases={8: 2, 9: 3},
        scratch_shapes=work(rows) + ends + [pltpu.VMEM((rows, half), bf)],
        compiler_params=params,
        cost_estimate=cost(0.5),
    )(blend, gain_own, odd, last, w, start, same, qs, ks, vs, peak, total, acc)
    got = lax.ppermute(theirs, "pb", swap_route)

    own_part = pl.pallas_call(
        own_part_kernel,
        out_shape=on_chip((n_ha, rows, part), f32),
        in_specs=[vm, vm],
        out_specs=vm,
        compiler_params=params,
        cost_estimate=pl.CostEstimate(
            flops=2 * rows * half * cols, bytes_accessed=8_000_000, transcendentals=0
        ),
    )(mine, w_own)

    def finish(lo, got):
        return pl.pallas_call(
            functools.partial(add_part_kernel, lo=lo),
            out_shape=(on_chip((rows, part), bf), on_chip((rows, part), bf)),
            in_specs=[vm, vm, vm],
            out_specs=(vm, vm),
            compiler_params=params,
            cost_estimate=pl.CostEstimate(
                flops=rows * half * cols, bytes_accessed=4_000_000, transcendentals=0
            ),
        )(got, w_oth, own_part)

    near_route = [(i, i ^ 1) for i in range(n_ha)]
    give, keep = finish(0, got)
    take = lax.ppermute(give, "ha", near_route)
    away = (keep.astype(f32) + take.astype(f32)).astype(bf)
    arrived = lax.ppermute(away, "ha", [(i, i ^ 2) for i in range(n_ha)])
    give, keep = finish(2, got)
    take = lax.ppermute(give, "ha", near_route)
    here = keep.astype(f32) + take.astype(f32)
    return (here + arrived.astype(f32)).astype(bf)


def per_device(queries, keys, values, theta, mix, gain, out_weight, turn_lengths):
    rows, feats = queries.shape
    heads = theta.shape[0]
    fits = rows == 128 and feats == 128 * heads and heads == 2 * GROUP
    n_pb, n_ha = lax.axis_size("pb"), lax.axis_size("ha")
    fits = fits and n_pb % 2 == 0 and n_ha == 4
    args = (queries, keys, values, theta, mix, gain, out_weight, turn_lengths)
    if not fits:
        return general_plan(*args)
    return paired_plan(*args)


def solution(mesh):
    return jax.shard_map(
        per_device,
        mesh=mesh,
        in_specs=(
            P("pb", "ha"),
            P("pb", "ha"),
            P("pb", "ha"),
            P("ha", None, None),
            P("ha", None),
            P("ha"),
            P("ha", None),
            P(),
        ),
        out_specs=P("pb", "ha"),
        check_vma=False,
    )
```

```python
import functools
import math

import jax
import jax.numpy as jnp
from jax import lax
from jax.experimental import pallas as pl
from jax.experimental.pallas import tpu as pltpu
from jax.sharding import PartitionSpec as P


GROUP = 4
QCONV = 6
KCONV = 11
MAXBACK = 5
HALO = 16
NEG = -1e30
FLOOR = -5e29
INSET = 16


def place():
    me = lax.axis_index("pb")
    side = lax.rem(me, 2)
    return side, me - side


def copy_all(copies, sems):
    started = []
    for n, (src, dst) in enumerate(copies):
        copy = pltpu.make_async_copy(src, dst, sems.at[n])
        copy.start()
        started.append(copy)
    for copy in started:
        copy.wait()


def first_kernel(q_ref, k_ref, v_ref, own_kv, sems):
    side, _ = place()
    rows = q_ref.shape[0]
    half = q_ref.shape[1] // 2
    own = pl.ds(pl.multiple_of(side * half, half), half)
    copy_all(
        [
            (k_ref.at[:, own], own_kv.at[HALO : HALO + rows, :]),
            (v_ref.at[:, own], own_kv.at[HALO + rows : HALO + 2 * rows, :]),
            (q_ref.at[rows - HALO : rows, own], own_kv.at[0:HALO, :]),
        ],
        sems,
    )


def split_kernel(q_ref, k_ref, v_ref, own_q, oth_all, oth_kv, sems):
    side, _ = place()
    rows = q_ref.shape[0]
    half = q_ref.shape[1] // 2
    own = pl.ds(pl.multiple_of(side * half, half), half)
    oth = pl.ds(pl.multiple_of((1 - side) * half, half), half)
    copy_all(
        [
            (k_ref.at[:, oth], oth_kv.at[HALO : HALO + rows, :]),
            (v_ref.at[:, oth], oth_kv.at[HALO + rows : HALO + 2 * rows, :]),
            (q_ref.at[rows - HALO : rows, oth], oth_kv.at[0:HALO, :]),
            (q_ref.at[:, oth], oth_all.at[0:rows, :]),
            (k_ref.at[:, oth], oth_all.at[rows : 2 * rows, :]),
            (v_ref.at[:, oth], oth_all.at[2 * rows : 3 * rows, :]),
            (q_ref.at[:, own], own_q),
        ],
        sems,
    )


def prep_kernel(
    len_ref, theta_ref, mix_ref, gain_ref, out_weight,
    w_ref, start_ref, same_ref, w_own, blend_ref, gain_out, sems, *, scale
):
    reach = (KCONV - 1) // 2
    width = 128
    side_here, first = place()
    copies = load_weights(out_weight, w_own, side_here, sems)
    base = side_here * GROUP
    first_row = first * ((start_ref.shape[0] - HALO) // 2)
    diff = lax.broadcasted_iota(jnp.int32, (width, width), 1) - lax.broadcasted_iota(
        jnp.int32, (width, width), 0
    )

    def body(step, carry):
        h = step // (QCONV // 2)
        q = step % (QCONV // 2)
        for side in range(2):
            lo = jnp.zeros((width, width), jnp.float32)
            hi = jnp.zeros((width, width), jnp.float32)
            tap = 2 * q + side
            for b in range(-reach, reach + 1):
                t = theta_ref[tap, base + h, b + reach] * scale
                lo = jnp.where(diff == b - INSET, t, lo)
                hi = jnp.where(diff == b + width - INSET, t, hi)
            w_ref[step, 0:width, side * width : (side + 1) * width] = lo.astype(jnp.bfloat16)
            w_ref[step, width : 2 * width, side * width : (side + 1) * width] = hi.astype(
                jnp.bfloat16
            )
        return carry

    lax.fori_loop(0, GROUP * QCONV // 2, body, 0)
    for p in range(GROUP):
        for h in range(GROUP):
            n = p * GROUP + h
            blend_ref[n : n + 1, :] = jnp.full((1, width), mix_ref[p, base + h], jnp.float32)
    half = gain_out.shape[1]
    gain_out[...] = gain_ref[:, pl.ds(pl.multiple_of(side_here * half, half), half)]
    shape = start_ref.shape
    row = first_row - HALO + lax.broadcasted_iota(jnp.int32, shape, 0)
    start = jnp.zeros(shape, jnp.int32)
    begin = jnp.int32(0)
    for n in range(len_ref.shape[0]):
        start = jnp.where(row >= begin, begin, start)
        begin = begin + len_ref[n]
    start_ref[...] = start
    for a in range(1, QCONV):
        same_ref[a - 1] = (row[HALO:] - a >= start[HALO:]).astype(jnp.float32)
    for copy in copies:
        copy.wait()


def window_masks(col0, first_row, row0, n_rows, start, score_ok, bias):
    n_ext = n_rows + HALO
    lane = lax.broadcasted_iota(jnp.int32, (1, 128), 1)
    start_ext = start[pl.ds(row0, n_ext), :]
    row_ext = first_row + row0 - HALO + lax.broadcasted_iota(jnp.int32, (n_ext, 128), 0)
    for t in range(3):
        col = col0 + t * 128 + lane
        ok = (col >= start_ext) & (col <= row_ext)
        score_ok[t] = jnp.where(ok, 1.0, 0.0)
    for t in range(2):
        col = col0 + INSET + t * 128 + lane
        ok = (col >= start_ext[HALO:]) & (col <= row_ext[HALO:])
        bias[t] = jnp.where(ok, 0.0, NEG)


def reaches(start, row0, col0):
    return jnp.min(start[row0 + HALO : row0 + HALO + 8, :]) < col0 + INSET + 256


def one_window(at, row0, n_rows, qs, ks, vs, w, same, work, state, result):
    score_ok, bias, lhs, ps, probs, factors = work
    peak, total, acc = state
    peak_out, total_out, acc_out = result
    n_ext = n_rows + HALO
    dh = 128
    n_q = QCONV // 2
    step = 64

    def scores(h):
        cols = slice(h * dh, (h + 1) * dh)
        buf = h % 2
        s = lax.dot_general(
            qs[pl.ds(row0, n_ext), cols],
            ks[pl.ds(at, 384), cols],
            (((1,), (1,)), ((), ())),
            preferred_element_type=jnp.float32,
        )
        for t in range(3):
            piece = jnp.where(score_ok[t] > 0.0, s[:, t * 128 : (t + 1) * 128], 0.0)
            piece = piece.astype(jnp.bfloat16)
            if t < 2:
                lhs[buf, 0:n_ext, t * 128 : (t + 1) * 128] = piece
            if t > 0:
                lhs[buf, n_ext : 2 * n_ext, (t - 1) * 128 : t * 128] = piece

    def taps(h, q):
        buf = h % 2
        pair = jnp.dot(lhs[buf], w[h * n_q + q], preferred_element_type=jnp.float32)
        ps[buf, 2 * q] = pair[:, 0:128]
        ps[buf, 2 * q + 1] = pair[:, 128:256]

    def weigh(h, r):
        buf = h % 2
        rows = pl.ds(row0 + r, step)
        keep = [same[a - 1, rows, :] > 0.0 for a in range(1, QCONV)]
        parts = []
        for t in range(2):
            base = t * n_ext + HALO + r
            conv = ps[buf, 0, base : base + step, :] + bias[t, r : r + step, :]
            for a in range(1, QCONV):
                conv = conv + jnp.where(keep[a - 1], ps[buf, a, base - a : base - a + step, :], 0.0)
            parts.append(conv)
        old = peak[h, rows, :]
        top = jnp.max(jnp.maximum(parts[0], parts[1]), axis=1, keepdims=True)
        new = jnp.maximum(old, top)
        ws = [jnp.exp(c - new) for c in parts]
        factor = jnp.exp(old - new)
        if peak_out is not None:
            peak_out[h, rows, :] = new
        out_rows = rows if peak_out is not None else pl.ds(r, step)
        total_out[h, out_rows, :] = total[h, rows, :] * factor + jnp.sum(
            ws[0] + ws[1], axis=1, keepdims=True
        )
        factors[buf, r : r + step, :] = factor
        for t in range(2):
            probs[buf, r : r + step, t * 128 : (t + 1) * 128] = ws[t].astype(jnp.bfloat16)

    def gather(h):
        buf = h % 2
        out_rows = pl.ds(row0, n_rows) if peak_out is not None else pl.ds(0, n_rows)
        upd = jnp.dot(
            probs[buf], vs[pl.ds(at + INSET, 256), :], preferred_element_type=jnp.float32
        )
        factor = factors[buf]
        for t in range(GROUP):
            c = slice(t * dh, (t + 1) * dh)
            acc_out[h, out_rows, c] = acc[h, pl.ds(row0, n_rows), c] * factor + upd[:, c]

    chunks = list(range(0, n_rows, step))
    scores(0)
    for q in range(n_q):
        taps(0, q)
    for h in range(GROUP):
        more = h + 1 < GROUP
        if more:
            scores(h + 1)
        for n in range(max(len(chunks), n_q)):
            if n < len(chunks):
                weigh(h, chunks[n])
            if more and n < n_q:
                taps(h + 1, n)
        gather(h)


def put(src, lo, ks, vs, blk):
    rows = (src.shape[0] - lo) // 2
    at = pl.ds(pl.multiple_of(blk * rows, rows), rows)
    ks[at, :] = src[lo : lo + rows, :]
    vs[at, :] = src[lo + rows : lo + 2 * rows, :]


def load_weights(out_weight, dst, who, sems, skip=0):
    half, part = dst.shape[1:]
    ha = lax.axis_index("ha")
    core = lax.rem(ha, 2)
    pair = ha - core
    away = 2 - pair
    order = (away + 1 - core, away + core, pair + 1 - core, ha)
    copies = []
    for n in range(dst.shape[0]):
        rows = pl.ds(pl.multiple_of(who * half, half), half)
        cols = pl.ds(pl.multiple_of(order[skip + n] * part, part), part)
        copy = pltpu.make_async_copy(out_weight.at[rows, cols], dst.at[n], sems.at[n])
        copy.start()
        copies.append(copy)
    return copies


def far_source_kernel(own_kv, swap, out_ref):
    side, _ = place()
    rows = out_ref.shape[0] // 2

    @pl.when(side == 0)
    def _():
        out_ref[...] = swap[rows : 3 * rows, :]

    @pl.when(side == 1)
    def _():
        out_ref[...] = own_kv[HALO : HALO + 2 * rows, :]


def own_kernel(
    own_q, own_kv, swap, w, start, same,
    qs, ks, vs, peak, total, acc, score_ok, bias, lhs, ps, probs, factors
):
    rows, half = own_q.shape
    side, first = place()
    first_row = first * rows
    qs[pl.ds(pl.multiple_of(HALO + side * rows, HALO), rows), :] = own_q[...]
    qs[pl.ds(pl.multiple_of(HALO + (1 - side) * rows, HALO), rows), :] = swap[0:rows, :]

    qs[0:HALO, :] = jnp.zeros((HALO, half), jnp.bfloat16)
    zero = jnp.zeros((rows, half), jnp.bfloat16)
    for blk in (0, 1, 8):
        ks[blk * rows : (blk + 1) * rows, :] = zero
        vs[blk * rows : (blk + 1) * rows, :] = zero
    put(own_kv, HALO, ks, vs, 6 + side)
    put(swap, rows, ks, vs, 7 - side)
    peak[...] = jnp.full(peak.shape, FLOOR, jnp.float32)
    total[...] = jnp.zeros(total.shape, jnp.float32)
    acc[...] = jnp.zeros(acc.shape, jnp.float32)
    state = (peak, total, acc)
    window_masks(first_row, first_row, 0, 2 * rows, start, score_ok, bias)
    one_window(
        6 * rows, 0, 2 * rows, qs, ks, vs, w, same,
        (score_ok, bias, lhs, ps, probs, factors), state, state,
    )


def next_kernel(
    pa, pb, w, start, same, qs_in, ks_in, vs_in, peak_in, total_in, acc_in,
    qs, ks, vs, peak, total, acc, score_ok, bias, lhs, ps, probs, factors
):
    rows = (qs.shape[0] - HALO) // 2
    side, first = place()
    first_row = first * rows
    put(pa, HALO, ks, vs, 4 + side)
    put(pb, HALO, ks, vs, 5 - side)

    @pl.when(side == 0)
    def _():
        qs[0:HALO, :] = pb[0:HALO, :]

    @pl.when(side == 1)
    def _():
        qs[0:HALO, :] = pa[0:HALO, :]

    state = (peak, total, acc)
    window_masks(first_row - 2 * rows, first_row, 0, 2 * rows, start, score_ok, bias)
    one_window(
        4 * rows, 0, 2 * rows, qs, ks, vs, w, same,
        (score_ok, bias, lhs, ps, probs, factors), state, state,
    )


def mid_kernel(
    fa, fb, w, start, same, qs, ks_in, vs_in, peak_in, total_in, acc_in,
    ks, vs, peak, total, acc, score_ok, bias, lhs, ps, probs, factors
):
    rows = (qs.shape[0] - HALO) // 2
    side, first = place()
    first_row = first * rows
    put(fa, 0, ks, vs, 2 + side)
    put(fb, 0, ks, vs, 3 - side)
    state = (peak, total, acc)

    @pl.when(reaches(start, 0, first_row - 4 * rows))
    def _():
        window_masks(first_row - 4 * rows, first_row, 0, 2 * rows, start, score_ok, bias)
        one_window(
            2 * rows, 0, 2 * rows, qs, ks, vs, w, same,
            (score_ok, bias, lhs, ps, probs, factors), state, state,
        )


def finish_rows(
    mix_ref, gain_ref, row0, out_ref, ks, vs, w, start, same, qs, peak, total, acc,
    score_ok, bias, lhs, ps, probs, factors, total_end, acc_end
):
    rows, half = out_ref.shape
    _, first = place()
    first_row = first * rows
    dh = half // GROUP
    needed = reaches(start, row0, first_row - 6 * rows)

    @pl.when(needed)
    def _():
        window_masks(first_row - 6 * rows, first_row, row0, rows, start, score_ok, bias)
        one_window(
            0, row0, rows, qs, ks, vs, w, same, (score_ok, bias, lhs, ps, probs, factors),
            (peak, total, acc), (None, total_end, acc_end),
        )

    @pl.when(jnp.logical_not(needed))
    def _():
        total_end[...] = total[:, row0 : row0 + rows, :]
        acc_end[...] = acc[:, row0 : row0 + rows, :]

    inverse = [1.0 / total_end[p] for p in range(GROUP)]
    for h in range(GROUP):
        cols = slice(h * dh, (h + 1) * dh)
        out = jnp.zeros((rows, dh), jnp.float32)
        for p in range(GROUP):
            n = p * GROUP + h
            out = out + mix_ref[n : n + 1, :] * (acc_end[p, :, cols] * inverse[p])
        mean_sq = jnp.mean(out * out, axis=1, keepdims=True)
        out_ref[:, cols] = (out * lax.rsqrt(mean_sq + 1e-06) * gain_ref[:, cols]).astype(
            jnp.bfloat16
        )


def odd_kernel(
    mix_ref, gain_ref, w, start, same, qs, ks, vs, peak, total, acc,
    out_ref, score_ok, bias, lhs, ps, probs, factors, total_end, acc_end
):
    finish_rows(
        mix_ref, gain_ref, out_ref.shape[0], out_ref, ks, vs, w, start, same, qs, peak, total,
        acc, score_ok, bias, lhs, ps, probs, factors, total_end, acc_end,
    )


def even_kernel(
    mix_ref, gain_ref, odd_ref, last, w, start, same, qs, ks_in, vs_in, peak, total, acc,
    mine_ref, theirs_ref, ks, vs,
    score_ok, bias, lhs, ps, probs, factors, total_end, acc_end, even_ref
):
    side, _ = place()
    put(last, 0, ks, vs, 1)
    finish_rows(
        mix_ref, gain_ref, 0, even_ref, ks, vs, w, start, same, qs, peak, total,
        acc, score_ok, bias, lhs, ps, probs, factors, total_end, acc_end,
    )

    @pl.when(side == 0)
    def _():
        mine_ref[...] = even_ref[...]
        theirs_ref[...] = odd_ref[...]

    @pl.when(side == 1)
    def _():
        mine_ref[...] = odd_ref[...]
        theirs_ref[...] = even_ref[...]


def own_part_kernel(x_ref, w_ref, out_weight, out_ref, w_far, sems):
    side, _ = place()
    copies = load_weights(out_weight, w_far, 1 - side, sems)
    for n in range(w_ref.shape[0]):
        out_ref[n] = jnp.dot(x_ref[...], w_ref[n], preferred_element_type=jnp.float32)
    for copy in copies:
        copy.wait()


def late_part_kernel(x_ref, out_weight, part_ref, give_ref, keep_ref, w_near, sems):
    side, _ = place()
    for copy in load_weights(out_weight, w_near, 1 - side, sems, skip=2):
        copy.wait()
    add_part_kernel(x_ref, w_near, part_ref, give_ref, keep_ref, lo=2)


def add_part_kernel(x_ref, w_ref, part_ref, give_ref, keep_ref, *, lo):
    for n, out_ref in enumerate((give_ref, keep_ref)):
        out = jnp.dot(x_ref[...], w_ref[n], preferred_element_type=jnp.float32)
        out_ref[...] = (out + part_ref[lo + n]).astype(jnp.bfloat16)


def from_behind(block, axis, distance):
    devices = range(lax.axis_size(axis))
    route = [(i - distance, i) for i in devices if i - distance in devices]
    return lax.ppermute(block, axis, route)


def conv_block(scores, theta_part, row_pos, row_start, col_pos, out_cols):
    rim_rows = QCONV - 1
    count_rows = row_pos.shape[0]
    conv_sum = jnp.zeros((scores.shape[0], count_rows, out_cols), jnp.float32)
    above_start = col_pos[None, :] >= row_start[:, None]
    for offset_q in range(QCONV):
        allowed = above_start & (col_pos[None, :] <= row_pos[:, None] - offset_q)
        taken_rows = jnp.where(
            allowed[None],
            scores[:, rim_rows - offset_q : rim_rows - offset_q + count_rows, :],
            jnp.float32(0.0),
        )
        for offset_k in range(KCONV):
            conv_sum = (
                conv_sum
                + theta_part[:, offset_q, KCONV - 1 - offset_k][:, None, None]
                * taken_rows[:, :, offset_k : offset_k + out_cols]
            )
    return conv_sum


def general_plan(queries, keys, values, theta, mix, gain, out_weight, turn_lengths):
    tile_rows = queries.shape[0]
    feature_cols = queries.shape[1]
    local_heads = theta.shape[0]
    head_size = feature_cols // local_heads
    groups = local_heads // GROUP
    group_cols = GROUP * head_size
    rim_rows = QCONV - 1
    key_reach = (KCONV - 1) // 2
    tile_index = lax.axis_index("pb")
    first_row = tile_index * tile_rows
    starts = jnp.cumsum(turn_lengths) - turn_lengths
    row_pos = first_row + jnp.arange(tile_rows, dtype=jnp.int32)
    row_start = jnp.max(jnp.where(starts[None, :] <= row_pos[:, None], starts[None, :], 0), axis=1)
    earlier = from_behind(queries[tile_rows - rim_rows :], "pb", 1)
    query_ext = jnp.concatenate([earlier, queries], 0).reshape(
        tile_rows + rim_rows, local_heads, head_size
    )
    kv_pair = jnp.stack([keys, values], 0)
    window = kv_pair[None]
    while window.shape[0] < MAXBACK + 1:
        have_count = window.shape[0]
        take_count = min(have_count, MAXBACK + 1 - have_count)
        moved_runs = from_behind(window[have_count - take_count :], "pb", have_count)
        window = jnp.concatenate([moved_runs, window], 0)
    key_span = (MAXBACK + 1) * tile_rows
    key_win = window[:, 0].reshape(key_span, feature_cols)
    val_win = window[:, 1].reshape(key_span, feature_cols)
    key_pad = jnp.pad(key_win, ((key_reach, key_reach), (0, 0))).reshape(
        key_span + 2 * key_reach, local_heads, head_size
    )
    key_base = first_row - MAXBACK * tile_rows
    score_scale = 1.0 / math.sqrt(head_size)
    state_carry = (
        jnp.full((local_heads, tile_rows), -1e30, jnp.float32),
        jnp.zeros((local_heads, tile_rows), jnp.float32),
        jnp.zeros((local_heads, tile_rows, group_cols), jnp.float32),
    )
    for block_num in range(MAXBACK + 1):
        block_row_peak, block_row_total, block_accumulated = state_carry
        lower = block_num * tile_rows
        key_slice = key_pad[lower : lower + tile_rows + 2 * key_reach]
        scores = (
            jnp.einsum("rhd,chd->hrc", query_ext, key_slice, preferred_element_type=jnp.float32)
            * score_scale
        )
        col_pos = (
            key_base + lower - key_reach + jnp.arange(tile_rows + 2 * key_reach, dtype=jnp.int32)
        )
        conv_sum = conv_block(scores, theta, row_pos, row_start, col_pos, tile_rows)
        key_pos = key_base + lower + jnp.arange(tile_rows, dtype=jnp.int32)
        keep_mask = (key_pos[None, :] >= row_start[:, None]) & (
            key_pos[None, :] <= row_pos[:, None]
        )
        masked = jnp.where(keep_mask[None], conv_sum, jnp.float32(-1e30))
        new_peak = jnp.maximum(block_row_peak, jnp.max(masked, axis=-1))
        weights = jnp.where(
            keep_mask[None], jnp.exp(conv_sum - new_peak[..., None]), jnp.float32(0.0)
        )
        factor = jnp.exp(block_row_peak - new_peak)
        new_total = block_row_total * factor + jnp.sum(weights, axis=-1)
        prob_bf = weights.astype(jnp.bfloat16).reshape(groups, GROUP, tile_rows, tile_rows)
        val_block = val_win[lower : lower + tile_rows].reshape(tile_rows, groups, group_cols)
        update = jnp.einsum(
            "gpij,jgc->gpic", prob_bf, val_block, preferred_element_type=jnp.float32
        )
        update = update.reshape(local_heads, tile_rows, group_cols)
        state_carry = (new_peak, new_total, block_accumulated * factor[..., None] + update)
    _, row_total, accumulated = state_carry
    normalized = (accumulated / row_total[..., None]).reshape(
        groups, GROUP, tile_rows, GROUP, head_size
    )
    mix_grid = mix.reshape(groups, GROUP, GROUP)
    head_out = jnp.einsum("gkp,gpikd->gikd", mix_grid, normalized)
    head_out = jnp.transpose(head_out, (1, 0, 2, 3)).reshape(tile_rows, local_heads, head_size)
    mean_sq = jnp.mean(head_out * head_out, axis=-1, keepdims=True)
    normed = (
        (head_out * lax.rsqrt(mean_sq + 1e-06) * gain.reshape(local_heads, head_size))
        .reshape(tile_rows, feature_cols)
        .astype(jnp.bfloat16)
    )
    summed = lax.psum_scatter(
        lax.dot_general(
            out_weight, normed, (((0,), (1,)), ((), ())), preferred_element_type=jnp.float32
        ).astype(jnp.bfloat16),
        "ha",
        scatter_dimension=0,
        tiled=True,
    ).astype(jnp.float32)
    return summed.T.astype(jnp.bfloat16)


def paired_plan(queries, keys, values, theta, mix, gain, out_weight, turn_lengths):
    rows, feats = queries.shape
    half = feats // 2
    heads = theta.shape[0]
    dh = feats // heads
    n_pb = lax.axis_size("pb")
    n_ha = lax.axis_size("ha")
    vm = pl.BlockSpec(memory_space=pltpu.VMEM)
    sm = pl.BlockSpec(memory_space=pltpu.SMEM)
    hbm = pl.BlockSpec(memory_space=pltpu.HBM)
    stay = functools.partial(pltpu.with_memory_space_constraint, memory_space=pltpu.HBM)
    small = pltpu.CompilerParams(vmem_limit_bytes=8 * 1024 * 1024)
    bf = jnp.bfloat16
    f32 = jnp.float32
    kv_rows = 2 * rows + HALO
    n_rows = 2 * rows
    n_ext = n_rows + HALO
    on_chip = pltpu.VMEM
    params = pltpu.CompilerParams(vmem_limit_bytes=24 * 1024 * 1024)

    inputs = (stay(queries), stay(keys), stay(values))
    own_kv = pl.pallas_call(
        first_kernel,
        out_shape=on_chip((kv_rows, half), bf),
        in_specs=[hbm] * 3,
        out_specs=vm,
        scratch_shapes=[pltpu.SemaphoreType.DMA((3,))],
        compiler_params=small,
    )(*inputs)
    own_q, oth_all, oth_kv = pl.pallas_call(
        split_kernel,
        out_shape=(
            on_chip((rows, half), bf),
            on_chip((3 * rows, half), bf),
            on_chip((kv_rows, half), bf),
        ),
        in_specs=[hbm] * 3,
        out_specs=(vm, vm, vm),
        scratch_shapes=[pltpu.SemaphoreType.DMA((7,))],
        compiler_params=small,
    )(*inputs)

    pairs = range(n_pb)
    up = [(i, i + 2) for i in pairs if i + 2 < n_pb]
    cross = [(i, (i ^ 1) + 2) for i in pairs if (i ^ 1) + 2 < n_pb]
    swap_route = [(i, i ^ 1) for i in pairs]
    far = [(i, i + MAXBACK + 1) for i in pairs if i + MAXBACK + 1 < n_pb]

    pa = lax.ppermute(own_kv, "pb", up)
    pbk = lax.ppermute(oth_kv, "pb", cross)
    swap = lax.ppermute(oth_all, "pb", swap_route)

    n_pair = GROUP * QCONV // 2
    cols = out_weight.shape[1]
    part = cols // n_ha
    weights = on_chip((n_ha, half, part), bf)
    heavy = stay(out_weight)
    prep_params = pltpu.CompilerParams(vmem_limit_bytes=16 * 1024 * 1024)
    w, start, same, w_own, blend, gain_own = pl.pallas_call(
        functools.partial(prep_kernel, scale=1.0 / math.sqrt(dh)),
        out_shape=(
            on_chip((n_pair, 256, 256), bf),
            on_chip((n_ext, 128), jnp.int32),
            on_chip((QCONV - 1, n_rows, 128), f32),
            weights,
            on_chip((GROUP * GROUP, 128), f32),
            on_chip((1, half), f32),
        ),
        in_specs=[sm, sm, sm, vm, hbm],
        out_specs=(vm,) * 6,
        scratch_shapes=[pltpu.SemaphoreType.DMA((n_ha,))],
        compiler_params=prep_params,
        cost_estimate=pl.CostEstimate(
            flops=20_000_000, bytes_accessed=2_400_000, transcendentals=0
        ),
    )(stay(turn_lengths), stay(theta.transpose(1, 0, 2)), stay(mix.T), stay(gain.reshape(1, -1)), heavy)
    pa, w = lax.optimization_barrier((pa, w))
    fa = lax.ppermute(pa[HALO:], "pb", up)
    fb = lax.ppermute(pbk[HALO:], "pb", up)

    def state(make):
        return (
            make((GROUP, n_rows, 128), f32),
            make((GROUP, n_rows, 128), f32),
            make((GROUP, n_rows, half), f32),
        )

    def work(count):
        ext = count + HALO
        return [
            pltpu.VMEM((3, ext, 128), f32),
            pltpu.VMEM((2, count, 128), f32),
            pltpu.VMEM((2, 2 * ext, 256), bf),
            pltpu.VMEM((2, QCONV, 2 * ext, 128), f32),
            pltpu.VMEM((2, count, 256), bf),
            pltpu.VMEM((2, count, 128), f32),
        ]

    def cost(n):
        return pl.CostEstimate(
            flops=int(n * 1_500_000_000),
            bytes_accessed=int(n * 6_000_000),
            transcendentals=int(n * 300_000),
        )

    some_weights = on_chip((2, half, part), bf)
    span = on_chip((9 * rows, half), bf)
    e_src = pl.pallas_call(
        far_source_kernel,
        out_shape=on_chip((2 * rows, half), bf),
        in_specs=[vm, vm],
        out_specs=vm,
        compiler_params=small,
    )(own_kv, swap)
    last = lax.ppermute(e_src, "pb", far)
    qs, ks, vs, peak, total, acc = pl.pallas_call(
        own_kernel,
        out_shape=(on_chip((n_ext, half), bf), span, span)
        + state(on_chip)
,
        in_specs=[vm] * 6,
        out_specs=(vm,) * 6,
        scratch_shapes=work(n_rows),
        compiler_params=params,
        cost_estimate=cost(1),
    )(own_q, own_kv, swap, w, start, same)
    qs, ks, vs, peak, total, acc = pl.pallas_call(
        next_kernel,
        out_shape=(on_chip((n_ext, half), bf), span, span) + state(on_chip),
        in_specs=[vm] * 11,
        out_specs=(vm,) * 6,
        input_output_aliases={5: 0, 6: 1, 7: 2, 8: 3, 9: 4, 10: 5},
        scratch_shapes=work(n_rows),
        compiler_params=params,
        cost_estimate=cost(1),
    )(pa, pbk, w, start, same, qs, ks, vs, peak, total, acc)
    ks, vs, peak, total, acc = pl.pallas_call(
        mid_kernel,
        out_shape=(span, span) + state(on_chip),
        in_specs=[vm] * 11,
        out_specs=(vm,) * 5,
        input_output_aliases={6: 0, 7: 1, 8: 2, 9: 3, 10: 4},
        scratch_shapes=work(n_rows),
        compiler_params=params,
        cost_estimate=cost(1),
    )(fa, fb, w, start, same, qs, ks, vs, peak, total, acc)
    ends = [pltpu.VMEM((GROUP, rows, 128), f32), pltpu.VMEM((GROUP, rows, half), f32)]
    odd = pl.pallas_call(
        odd_kernel,
        out_shape=on_chip((rows, half), bf),
        in_specs=[vm] * 11,
        out_specs=vm,
        scratch_shapes=work(rows) + ends,
        compiler_params=params,
        cost_estimate=cost(0.5),
    )(blend, gain_own, w, start, same, qs, ks, vs, peak, total, acc)
    last, odd = lax.optimization_barrier((last, odd))
    mine, theirs, _, _ = pl.pallas_call(
        even_kernel,
        out_shape=(on_chip((rows, half), bf),) * 2 + (span, span),
        in_specs=[vm] * 13,
        out_specs=(vm,) * 4,
        input_output_aliases={8: 2, 9: 3},
        scratch_shapes=work(rows) + ends + [pltpu.VMEM((rows, half), bf)],
        compiler_params=params,
        cost_estimate=cost(0.5),
    )(blend, gain_own, odd, last, w, start, same, qs, ks, vs, peak, total, acc)
    got = lax.ppermute(theirs, "pb", swap_route)

    own_part, w_far = pl.pallas_call(
        own_part_kernel,
        out_shape=(on_chip((n_ha, rows, part), f32), some_weights),
        in_specs=[vm, vm, hbm],
        out_specs=(vm, vm),
        scratch_shapes=[pltpu.SemaphoreType.DMA((2,))],
        compiler_params=params,
        cost_estimate=pl.CostEstimate(
            flops=2 * rows * half * cols, bytes_accessed=8_000_000, transcendentals=0
        ),
    )(mine, w_own, heavy)
    halves = (on_chip((rows, part), bf), on_chip((rows, part), bf))
    half_cost = pl.CostEstimate(
        flops=rows * half * cols, bytes_accessed=4_000_000, transcendentals=0
    )

    near_route = [(i, i ^ 1) for i in range(n_ha)]
    give, keep = pl.pallas_call(
        functools.partial(add_part_kernel, lo=0),
        out_shape=halves,
        in_specs=[vm, vm, vm],
        out_specs=(vm, vm),
        compiler_params=params,
        cost_estimate=half_cost,
    )(got, w_far, own_part)
    take = lax.ppermute(give, "ha", near_route)
    away = (keep.astype(f32) + take.astype(f32)).astype(bf)
    arrived = lax.ppermute(away, "ha", [(i, i ^ 2) for i in range(n_ha)])
    give, keep = pl.pallas_call(
        late_part_kernel,
        out_shape=halves,
        in_specs=[vm, hbm, vm],
        out_specs=(vm, vm),
        scratch_shapes=[pltpu.VMEM((2, half, part), bf), pltpu.SemaphoreType.DMA((2,))],
        compiler_params=params,
        cost_estimate=half_cost,
    )(got, heavy, own_part)
    take = lax.ppermute(give, "ha", near_route)
    here = keep.astype(f32) + take.astype(f32)
    return (here + arrived.astype(f32)).astype(bf)


def per_device(queries, keys, values, theta, mix, gain, out_weight, turn_lengths):
    rows, feats = queries.shape
    heads = theta.shape[0]
    fits = rows == 128 and feats == 128 * heads and heads == 2 * GROUP
    n_pb, n_ha = lax.axis_size("pb"), lax.axis_size("ha")
    fits = fits and n_pb % 2 == 0 and n_ha == 4
    args = (queries, keys, values, theta, mix, gain, out_weight, turn_lengths)
    if not fits:
        return general_plan(*args)
    return paired_plan(*args)


def solution(mesh):
    return jax.shard_map(
        per_device,
        mesh=mesh,
        in_specs=(
            P("pb", "ha"),
            P("pb", "ha"),
            P("pb", "ha"),
            P("ha", None, None),
            P("ha", None),
            P("ha"),
            P("ha", None),
            P(),
        ),
        out_specs=P("pb", "ha"),
        check_vma=False,
    )
```

```python
import functools
import math

import jax
import jax.numpy as jnp
from jax import lax
from jax.experimental import pallas as pl
from jax.experimental.pallas import tpu as pltpu
from jax.sharding import PartitionSpec as P


GROUP = 4
QCONV = 6
KCONV = 11
MAXBACK = 5
HALO = 16
TAIL = 8
NEG = -1e30
FLOOR = -5e29
INSET = 16


def place():
    me = lax.axis_index("pb")
    side = lax.rem(me, 2)
    return side, me - side


def copy_all(copies, sems):
    started = []
    for n, (src, dst) in enumerate(copies):
        copy = pltpu.make_async_copy(src, dst, sems.at[n])
        copy.start()
        started.append(copy)
    for copy in started:
        copy.wait()


def first_kernel(q_ref, k_ref, v_ref, own_kv, sems):
    side, _ = place()
    rows = q_ref.shape[0]
    half = q_ref.shape[1] // 2
    own = pl.ds(pl.multiple_of(side * half, half), half)
    copy_all(
        [
            (k_ref.at[:, own], own_kv.at[TAIL : TAIL + rows, :]),
            (v_ref.at[:, own], own_kv.at[TAIL + rows : TAIL + 2 * rows, :]),
            (q_ref.at[rows - TAIL : rows, own], own_kv.at[0:TAIL, :]),
        ],
        sems,
    )


def split_kernel(q_ref, k_ref, v_ref, own_q, oth_all, oth_kv, sems):
    side, _ = place()
    rows = q_ref.shape[0]
    half = q_ref.shape[1] // 2
    own = pl.ds(pl.multiple_of(side * half, half), half)
    oth = pl.ds(pl.multiple_of((1 - side) * half, half), half)
    copy_all(
        [
            (k_ref.at[:, oth], oth_kv.at[TAIL : TAIL + rows, :]),
            (v_ref.at[:, oth], oth_kv.at[TAIL + rows : TAIL + 2 * rows, :]),
            (q_ref.at[rows - TAIL : rows, oth], oth_kv.at[0:TAIL, :]),
            (q_ref.at[:, oth], oth_all.at[0:rows, :]),
            (k_ref.at[:, oth], oth_all.at[rows : 2 * rows, :]),
            (v_ref.at[:, oth], oth_all.at[2 * rows : 3 * rows, :]),
            (q_ref.at[:, own], own_q),
        ],
        sems,
    )


def prep_kernel(
    len_ref, theta_ref, mix_ref, gain_ref, out_weight,
    w_ref, start_ref, same_ref, w_own, blend_ref, gain_out, sems, *, scale
):
    reach = (KCONV - 1) // 2
    width = 128
    side_here, first = place()
    copies = load_weights(out_weight, w_own, side_here, sems)
    base = side_here * GROUP
    first_row = first * ((start_ref.shape[0] - HALO) // 2)
    diff = lax.broadcasted_iota(jnp.int32, (width, width), 1) - lax.broadcasted_iota(
        jnp.int32, (width, width), 0
    )

    def body(step, carry):
        h = step // (QCONV // 2)
        q = step % (QCONV // 2)
        for side in range(2):
            lo = jnp.zeros((width, width), jnp.float32)
            hi = jnp.zeros((width, width), jnp.float32)
            tap = 2 * q + side
            for b in range(-reach, reach + 1):
                t = theta_ref[tap, base + h, b + reach] * scale
                lo = jnp.where(diff == b - INSET, t, lo)
                hi = jnp.where(diff == b + width - INSET, t, hi)
            w_ref[step, 0:width, side * width : (side + 1) * width] = lo.astype(jnp.bfloat16)
            w_ref[step, width : 2 * width, side * width : (side + 1) * width] = hi.astype(
                jnp.bfloat16
            )
        return carry

    lax.fori_loop(0, GROUP * QCONV // 2, body, 0)
    for p in range(GROUP):
        for h in range(GROUP):
            n = p * GROUP + h
            blend_ref[n : n + 1, :] = jnp.full((1, width), mix_ref[p, base + h], jnp.float32)
    half = gain_out.shape[1]
    gain_out[...] = gain_ref[:, pl.ds(pl.multiple_of(side_here * half, half), half)]
    shape = start_ref.shape
    row = first_row - HALO + lax.broadcasted_iota(jnp.int32, shape, 0)
    start = jnp.zeros(shape, jnp.int32)
    begin = jnp.int32(0)
    for n in range(len_ref.shape[0]):
        start = jnp.where(row >= begin, begin, start)
        begin = begin + len_ref[n]
    start_ref[...] = start
    for a in range(1, QCONV):
        same_ref[a - 1] = (row[HALO:] - a >= start[HALO:]).astype(jnp.float32)
    for copy in copies:
        copy.wait()


def window_masks(col0, first_row, row0, n_rows, start, score_ok, bias):
    n_ext = n_rows + HALO
    lane = lax.broadcasted_iota(jnp.int32, (1, 128), 1)
    start_ext = start[pl.ds(row0, n_ext), :]
    row_ext = first_row + row0 - HALO + lax.broadcasted_iota(jnp.int32, (n_ext, 128), 0)
    for t in range(3):
        col = col0 + t * 128 + lane
        ok = (col >= start_ext) & (col <= row_ext)
        score_ok[t] = jnp.where(ok, 1.0, 0.0)
    for t in range(2):
        col = col0 + INSET + t * 128 + lane
        ok = (col >= start_ext[HALO:]) & (col <= row_ext[HALO:])
        bias[t] = jnp.where(ok, 0.0, NEG)


def reaches(start, row0, col0):
    return jnp.min(start[row0 + HALO : row0 + HALO + 8, :]) < col0 + INSET + 256


def one_window(at, row0, n_rows, qs, ks, vs, w, same, work, state, result):
    score_ok, bias, lhs, ps, probs, factors = work
    peak, total, acc = state
    peak_out, total_out, acc_out = result
    n_ext = n_rows + HALO
    dh = 128
    n_q = QCONV // 2
    step = 64

    def scores(h):
        cols = slice(h * dh, (h + 1) * dh)
        buf = h % 2
        s = lax.dot_general(
            qs[pl.ds(row0, n_ext), cols],
            ks[pl.ds(at, 384), cols],
            (((1,), (1,)), ((), ())),
            preferred_element_type=jnp.float32,
        )
        for t in range(3):
            piece = jnp.where(score_ok[t] > 0.0, s[:, t * 128 : (t + 1) * 128], 0.0)
            piece = piece.astype(jnp.bfloat16)
            if t < 2:
                lhs[buf, 0:n_ext, t * 128 : (t + 1) * 128] = piece
            if t > 0:
                lhs[buf, n_ext : 2 * n_ext, (t - 1) * 128 : t * 128] = piece

    def taps(h, q):
        buf = h % 2
        pair = jnp.dot(lhs[buf], w[h * n_q + q], preferred_element_type=jnp.float32)
        ps[buf, 2 * q] = pair[:, 0:128]
        ps[buf, 2 * q + 1] = pair[:, 128:256]

    def weigh(h, r):
        buf = h % 2
        rows = pl.ds(row0 + r, step)
        keep = [same[a - 1, rows, :] > 0.0 for a in range(1, QCONV)]
        parts = []
        for t in range(2):
            base = t * n_ext + HALO + r
            conv = ps[buf, 0, base : base + step, :] + bias[t, r : r + step, :]
            for a in range(1, QCONV):
                conv = conv + jnp.where(keep[a - 1], ps[buf, a, base - a : base - a + step, :], 0.0)
            parts.append(conv)
        old = peak[h, rows, :]
        top = jnp.max(jnp.maximum(parts[0], parts[1]), axis=1, keepdims=True)
        new = jnp.maximum(old, top)
        ws = [jnp.exp(c - new) for c in parts]
        factor = jnp.exp(old - new)
        if peak_out is not None:
            peak_out[h, rows, :] = new
        out_rows = rows if peak_out is not None else pl.ds(r, step)
        total_out[h, out_rows, :] = total[h, rows, :] * factor + jnp.sum(
            ws[0] + ws[1], axis=1, keepdims=True
        )
        factors[buf, r : r + step, :] = factor
        for t in range(2):
            probs[buf, r : r + step, t * 128 : (t + 1) * 128] = ws[t].astype(jnp.bfloat16)

    def gather(h):
        buf = h % 2
        out_rows = pl.ds(row0, n_rows) if peak_out is not None else pl.ds(0, n_rows)
        upd = jnp.dot(
            probs[buf], vs[pl.ds(at + INSET, 256), :], preferred_element_type=jnp.float32
        )
        factor = factors[buf]
        for t in range(GROUP):
            c = slice(t * dh, (t + 1) * dh)
            acc_out[h, out_rows, c] = acc[h, pl.ds(row0, n_rows), c] * factor + upd[:, c]

    chunks = list(range(0, n_rows, step))
    scores(0)
    for q in range(n_q):
        taps(0, q)
    for h in range(GROUP):
        more = h + 1 < GROUP
        if more:
            scores(h + 1)
        for n in range(max(len(chunks), n_q)):
            if n < len(chunks):
                weigh(h, chunks[n])
            if more and n < n_q:
                taps(h + 1, n)
        gather(h)


def put(src, lo, ks, vs, blk):
    rows = (src.shape[0] - lo) // 2
    at = pl.ds(pl.multiple_of(blk * rows, rows), rows)
    ks[at, :] = src[lo : lo + rows, :]
    vs[at, :] = src[lo + rows : lo + 2 * rows, :]


def load_weights(out_weight, dst, who, sems, skip=0):
    half, part = dst.shape[1:]
    ha = lax.axis_index("ha")
    core = lax.rem(ha, 2)
    pair = ha - core
    away = 2 - pair
    order = (away + 1 - core, away + core, pair + 1 - core, ha)
    copies = []
    for n in range(dst.shape[0]):
        rows = pl.ds(pl.multiple_of(who * half, half), half)
        cols = pl.ds(pl.multiple_of(order[skip + n] * part, part), part)
        copy = pltpu.make_async_copy(out_weight.at[rows, cols], dst.at[n], sems.at[n])
        copy.start()
        copies.append(copy)
    return copies


def far_source_kernel(own_kv, swap, out_ref):
    side, _ = place()
    rows = out_ref.shape[0] // 2

    @pl.when(side == 0)
    def _():
        out_ref[...] = swap[rows : 3 * rows, :]

    @pl.when(side == 1)
    def _():
        out_ref[...] = own_kv[TAIL : TAIL + 2 * rows, :]


def own_kernel(
    own_q, own_kv, swap, w, start, same,
    qs, ks, vs, peak, total, acc, score_ok, bias, lhs, ps, probs, factors
):
    rows, half = own_q.shape
    side, first = place()
    first_row = first * rows
    qs[pl.ds(pl.multiple_of(HALO + side * rows, HALO), rows), :] = own_q[...]
    qs[pl.ds(pl.multiple_of(HALO + (1 - side) * rows, HALO), rows), :] = swap[0:rows, :]

    qs[0:HALO, :] = jnp.zeros((HALO, half), jnp.bfloat16)
    zero = jnp.zeros((rows, half), jnp.bfloat16)
    for blk in (0, 1, 8):
        ks[blk * rows : (blk + 1) * rows, :] = zero
        vs[blk * rows : (blk + 1) * rows, :] = zero
    put(own_kv, TAIL, ks, vs, 6 + side)
    put(swap, rows, ks, vs, 7 - side)
    peak[...] = jnp.full(peak.shape, FLOOR, jnp.float32)
    total[...] = jnp.zeros(total.shape, jnp.float32)
    acc[...] = jnp.zeros(acc.shape, jnp.float32)
    state = (peak, total, acc)
    window_masks(first_row, first_row, 0, 2 * rows, start, score_ok, bias)
    one_window(
        6 * rows, 0, 2 * rows, qs, ks, vs, w, same,
        (score_ok, bias, lhs, ps, probs, factors), state, state,
    )


def next_kernel(
    pa, pb, w, start, same, qs_in, ks_in, vs_in, peak_in, total_in, acc_in,
    qs, ks, vs, peak, total, acc, score_ok, bias, lhs, ps, probs, factors
):
    rows = (qs.shape[0] - HALO) // 2
    side, first = place()
    first_row = first * rows
    put(pa, TAIL, ks, vs, 4 + side)
    put(pb, TAIL, ks, vs, 5 - side)

    @pl.when(side == 0)
    def _():
        qs[HALO - TAIL : HALO, :] = pb[0:TAIL, :]

    @pl.when(side == 1)
    def _():
        qs[HALO - TAIL : HALO, :] = pa[0:TAIL, :]

    state = (peak, total, acc)
    window_masks(first_row - 2 * rows, first_row, 0, 2 * rows, start, score_ok, bias)
    one_window(
        4 * rows, 0, 2 * rows, qs, ks, vs, w, same,
        (score_ok, bias, lhs, ps, probs, factors), state, state,
    )


def mid_kernel(
    fa, fb, w, start, same, qs, ks_in, vs_in, peak_in, total_in, acc_in,
    ks, vs, peak, total, acc, score_ok, bias, lhs, ps, probs, factors
):
    rows = (qs.shape[0] - HALO) // 2
    side, first = place()
    first_row = first * rows
    put(fa, 0, ks, vs, 2 + side)
    put(fb, 0, ks, vs, 3 - side)
    state = (peak, total, acc)

    @pl.when(reaches(start, 0, first_row - 4 * rows))
    def _():
        window_masks(first_row - 4 * rows, first_row, 0, 2 * rows, start, score_ok, bias)
        one_window(
            2 * rows, 0, 2 * rows, qs, ks, vs, w, same,
            (score_ok, bias, lhs, ps, probs, factors), state, state,
        )


def finish_rows(
    mix_ref, gain_ref, row0, out_ref, ks, vs, w, start, same, qs, peak, total, acc,
    score_ok, bias, lhs, ps, probs, factors, total_end, acc_end
):
    rows, half = out_ref.shape
    _, first = place()
    first_row = first * rows
    dh = half // GROUP
    needed = reaches(start, row0, first_row - 6 * rows)

    @pl.when(needed)
    def _():
        window_masks(first_row - 6 * rows, first_row, row0, rows, start, score_ok, bias)
        one_window(
            0, row0, rows, qs, ks, vs, w, same, (score_ok, bias, lhs, ps, probs, factors),
            (peak, total, acc), (None, total_end, acc_end),
        )

    @pl.when(jnp.logical_not(needed))
    def _():
        total_end[...] = total[:, row0 : row0 + rows, :]
        acc_end[...] = acc[:, row0 : row0 + rows, :]

    inverse = [1.0 / total_end[p] for p in range(GROUP)]
    for h in range(GROUP):
        cols = slice(h * dh, (h + 1) * dh)
        out = jnp.zeros((rows, dh), jnp.float32)
        for p in range(GROUP):
            n = p * GROUP + h
            out = out + mix_ref[n : n + 1, :] * (acc_end[p, :, cols] * inverse[p])
        mean_sq = jnp.mean(out * out, axis=1, keepdims=True)
        out_ref[:, cols] = (out * lax.rsqrt(mean_sq + 1e-06) * gain_ref[:, cols]).astype(
            jnp.bfloat16
        )


def odd_kernel(
    mix_ref, gain_ref, w, start, same, qs, ks, vs, peak, total, acc,
    out_ref, score_ok, bias, lhs, ps, probs, factors, total_end, acc_end
):
    finish_rows(
        mix_ref, gain_ref, out_ref.shape[0], out_ref, ks, vs, w, start, same, qs, peak, total,
        acc, score_ok, bias, lhs, ps, probs, factors, total_end, acc_end,
    )


def even_kernel(
    mix_ref, gain_ref, odd_ref, last, w, start, same, qs, ks_in, vs_in, peak, total, acc,
    mine_ref, theirs_ref, ks, vs,
    score_ok, bias, lhs, ps, probs, factors, total_end, acc_end, even_ref
):
    side, _ = place()
    put(last, 0, ks, vs, 1)
    finish_rows(
        mix_ref, gain_ref, 0, even_ref, ks, vs, w, start, same, qs, peak, total,
        acc, score_ok, bias, lhs, ps, probs, factors, total_end, acc_end,
    )

    @pl.when(side == 0)
    def _():
        mine_ref[...] = even_ref[...]
        theirs_ref[...] = odd_ref[...]

    @pl.when(side == 1)
    def _():
        mine_ref[...] = odd_ref[...]
        theirs_ref[...] = even_ref[...]


def own_part_kernel(x_ref, w_ref, out_weight, out_ref, w_far, sems):
    side, _ = place()
    copies = load_weights(out_weight, w_far, 1 - side, sems)
    for n in range(w_ref.shape[0]):
        out_ref[n] = jnp.dot(x_ref[...], w_ref[n], preferred_element_type=jnp.float32)
    for copy in copies:
        copy.wait()


def one_part_kernel(x_ref, w_ref, part_ref, out_ref, *, n):
    out = jnp.dot(x_ref[...], w_ref[n], preferred_element_type=jnp.float32)
    out_ref[...] = (out + part_ref[n]).astype(jnp.bfloat16)


def late_part_kernel(x_ref, out_weight, part_ref, give_ref, keep_ref, w_near, sems):
    side, _ = place()
    for copy in load_weights(out_weight, w_near, 1 - side, sems, skip=2):
        copy.wait()
    add_part_kernel(x_ref, w_near, part_ref, give_ref, keep_ref, lo=2)


def add_part_kernel(x_ref, w_ref, part_ref, give_ref, keep_ref, *, lo):
    for n, out_ref in enumerate((give_ref, keep_ref)):
        out = jnp.dot(x_ref[...], w_ref[n], preferred_element_type=jnp.float32)
        out_ref[...] = (out + part_ref[lo + n]).astype(jnp.bfloat16)


def from_behind(block, axis, distance):
    devices = range(lax.axis_size(axis))
    route = [(i - distance, i) for i in devices if i - distance in devices]
    return lax.ppermute(block, axis, route)


def conv_block(scores, theta_part, row_pos, row_start, col_pos, out_cols):
    rim_rows = QCONV - 1
    count_rows = row_pos.shape[0]
    conv_sum = jnp.zeros((scores.shape[0], count_rows, out_cols), jnp.float32)
    above_start = col_pos[None, :] >= row_start[:, None]
    for offset_q in range(QCONV):
        allowed = above_start & (col_pos[None, :] <= row_pos[:, None] - offset_q)
        taken_rows = jnp.where(
            allowed[None],
            scores[:, rim_rows - offset_q : rim_rows - offset_q + count_rows, :],
            jnp.float32(0.0),
        )
        for offset_k in range(KCONV):
            conv_sum = (
                conv_sum
                + theta_part[:, offset_q, KCONV - 1 - offset_k][:, None, None]
                * taken_rows[:, :, offset_k : offset_k + out_cols]
            )
    return conv_sum


def general_plan(queries, keys, values, theta, mix, gain, out_weight, turn_lengths):
    tile_rows = queries.shape[0]
    feature_cols = queries.shape[1]
    local_heads = theta.shape[0]
    head_size = feature_cols // local_heads
    groups = local_heads // GROUP
    group_cols = GROUP * head_size
    rim_rows = QCONV - 1
    key_reach = (KCONV - 1) // 2
    tile_index = lax.axis_index("pb")
    first_row = tile_index * tile_rows
    starts = jnp.cumsum(turn_lengths) - turn_lengths
    row_pos = first_row + jnp.arange(tile_rows, dtype=jnp.int32)
    row_start = jnp.max(jnp.where(starts[None, :] <= row_pos[:, None], starts[None, :], 0), axis=1)
    earlier = from_behind(queries[tile_rows - rim_rows :], "pb", 1)
    query_ext = jnp.concatenate([earlier, queries], 0).reshape(
        tile_rows + rim_rows, local_heads, head_size
    )
    kv_pair = jnp.stack([keys, values], 0)
    window = kv_pair[None]
    while window.shape[0] < MAXBACK + 1:
        have_count = window.shape[0]
        take_count = min(have_count, MAXBACK + 1 - have_count)
        moved_runs = from_behind(window[have_count - take_count :], "pb", have_count)
        window = jnp.concatenate([moved_runs, window], 0)
    key_span = (MAXBACK + 1) * tile_rows
    key_win = window[:, 0].reshape(key_span, feature_cols)
    val_win = window[:, 1].reshape(key_span, feature_cols)
    key_pad = jnp.pad(key_win, ((key_reach, key_reach), (0, 0))).reshape(
        key_span + 2 * key_reach, local_heads, head_size
    )
    key_base = first_row - MAXBACK * tile_rows
    score_scale = 1.0 / math.sqrt(head_size)
    state_carry = (
        jnp.full((local_heads, tile_rows), -1e30, jnp.float32),
        jnp.zeros((local_heads, tile_rows), jnp.float32),
        jnp.zeros((local_heads, tile_rows, group_cols), jnp.float32),
    )
    for block_num in range(MAXBACK + 1):
        block_row_peak, block_row_total, block_accumulated = state_carry
        lower = block_num * tile_rows
        key_slice = key_pad[lower : lower + tile_rows + 2 * key_reach]
        scores = (
            jnp.einsum("rhd,chd->hrc", query_ext, key_slice, preferred_element_type=jnp.float32)
            * score_scale
        )
        col_pos = (
            key_base + lower - key_reach + jnp.arange(tile_rows + 2 * key_reach, dtype=jnp.int32)
        )
        conv_sum = conv_block(scores, theta, row_pos, row_start, col_pos, tile_rows)
        key_pos = key_base + lower + jnp.arange(tile_rows, dtype=jnp.int32)
        keep_mask = (key_pos[None, :] >= row_start[:, None]) & (
            key_pos[None, :] <= row_pos[:, None]
        )
        masked = jnp.where(keep_mask[None], conv_sum, jnp.float32(-1e30))
        new_peak = jnp.maximum(block_row_peak, jnp.max(masked, axis=-1))
        weights = jnp.where(
            keep_mask[None], jnp.exp(conv_sum - new_peak[..., None]), jnp.float32(0.0)
        )
        factor = jnp.exp(block_row_peak - new_peak)
        new_total = block_row_total * factor + jnp.sum(weights, axis=-1)
        prob_bf = weights.astype(jnp.bfloat16).reshape(groups, GROUP, tile_rows, tile_rows)
        val_block = val_win[lower : lower + tile_rows].reshape(tile_rows, groups, group_cols)
        update = jnp.einsum(
            "gpij,jgc->gpic", prob_bf, val_block, preferred_element_type=jnp.float32
        )
        update = update.reshape(local_heads, tile_rows, group_cols)
        state_carry = (new_peak, new_total, block_accumulated * factor[..., None] + update)
    _, row_total, accumulated = state_carry
    normalized = (accumulated / row_total[..., None]).reshape(
        groups, GROUP, tile_rows, GROUP, head_size
    )
    mix_grid = mix.reshape(groups, GROUP, GROUP)
    head_out = jnp.einsum("gkp,gpikd->gikd", mix_grid, normalized)
    head_out = jnp.transpose(head_out, (1, 0, 2, 3)).reshape(tile_rows, local_heads, head_size)
    mean_sq = jnp.mean(head_out * head_out, axis=-1, keepdims=True)
    normed = (
        (head_out * lax.rsqrt(mean_sq + 1e-06) * gain.reshape(local_heads, head_size))
        .reshape(tile_rows, feature_cols)
        .astype(jnp.bfloat16)
    )
    summed = lax.psum_scatter(
        lax.dot_general(
            out_weight, normed, (((0,), (1,)), ((), ())), preferred_element_type=jnp.float32
        ).astype(jnp.bfloat16),
        "ha",
        scatter_dimension=0,
        tiled=True,
    ).astype(jnp.float32)
    return summed.T.astype(jnp.bfloat16)


def paired_plan(queries, keys, values, theta, mix, gain, out_weight, turn_lengths):
    rows, feats = queries.shape
    half = feats // 2
    heads = theta.shape[0]
    dh = feats // heads
    n_pb = lax.axis_size("pb")
    n_ha = lax.axis_size("ha")
    vm = pl.BlockSpec(memory_space=pltpu.VMEM)
    sm = pl.BlockSpec(memory_space=pltpu.SMEM)
    hbm = pl.BlockSpec(memory_space=pltpu.HBM)
    stay = functools.partial(pltpu.with_memory_space_constraint, memory_space=pltpu.HBM)
    small = pltpu.CompilerParams(vmem_limit_bytes=8 * 1024 * 1024)
    bf = jnp.bfloat16
    f32 = jnp.float32
    kv_rows = 2 * rows + TAIL
    n_rows = 2 * rows
    n_ext = n_rows + HALO
    on_chip = pltpu.VMEM
    params = pltpu.CompilerParams(vmem_limit_bytes=24 * 1024 * 1024)

    inputs = (stay(queries), stay(keys), stay(values))
    own_kv = pl.pallas_call(
        first_kernel,
        out_shape=on_chip((kv_rows, half), bf),
        in_specs=[hbm] * 3,
        out_specs=vm,
        scratch_shapes=[pltpu.SemaphoreType.DMA((3,))],
        compiler_params=small,
    )(*inputs)
    own_q, oth_all, oth_kv = pl.pallas_call(
        split_kernel,
        out_shape=(
            on_chip((rows, half), bf),
            on_chip((3 * rows, half), bf),
            on_chip((kv_rows, half), bf),
        ),
        in_specs=[hbm] * 3,
        out_specs=(vm, vm, vm),
        scratch_shapes=[pltpu.SemaphoreType.DMA((7,))],
        compiler_params=small,
    )(*inputs)

    pairs = range(n_pb)
    up = [(i, i + 2) for i in pairs if i + 2 < n_pb]
    onward = [(i, j) for i, j in up if i >= 2]
    cross = [(i, (i ^ 1) + 2) for i in pairs if (i ^ 1) + 2 < n_pb]
    swap_route = [(i, i ^ 1) for i in pairs]
    far = [(i, i + MAXBACK + 1) for i in pairs if i + MAXBACK + 1 < n_pb]

    pa = lax.ppermute(own_kv, "pb", up)
    pbk = lax.ppermute(oth_kv, "pb", cross)
    swap = lax.ppermute(oth_all, "pb", swap_route)

    n_pair = GROUP * QCONV // 2
    cols = out_weight.shape[1]
    part = cols // n_ha
    weights = on_chip((n_ha, half, part), bf)
    heavy = stay(out_weight)
    prep_params = pltpu.CompilerParams(vmem_limit_bytes=16 * 1024 * 1024)
    w, start, same, w_own, blend, gain_own = pl.pallas_call(
        functools.partial(prep_kernel, scale=1.0 / math.sqrt(dh)),
        out_shape=(
            on_chip((n_pair, 256, 256), bf),
            on_chip((n_ext, 128), jnp.int32),
            on_chip((QCONV - 1, n_rows, 128), f32),
            weights,
            on_chip((GROUP * GROUP, 128), f32),
            on_chip((1, half), f32),
        ),
        in_specs=[sm, sm, sm, vm, hbm],
        out_specs=(vm,) * 6,
        scratch_shapes=[pltpu.SemaphoreType.DMA((n_ha,))],
        compiler_params=prep_params,
        cost_estimate=pl.CostEstimate(
            flops=20_000_000, bytes_accessed=2_400_000, transcendentals=0
        ),
    )(stay(turn_lengths), stay(theta.transpose(1, 0, 2)), stay(mix.T), stay(gain.reshape(1, -1)), heavy)
    pa, w = lax.optimization_barrier((pa, w))
    fa = lax.ppermute(pa[TAIL:], "pb", onward)
    fb = lax.ppermute(pbk[TAIL:], "pb", onward)

    def state(make):
        return (
            make((GROUP, n_rows, 128), f32),
            make((GROUP, n_rows, 128), f32),
            make((GROUP, n_rows, half), f32),
        )

    def work(count):
        ext = count + HALO
        return [
            pltpu.VMEM((3, ext, 128), f32),
            pltpu.VMEM((2, count, 128), f32),
            pltpu.VMEM((2, 2 * ext, 256), bf),
            pltpu.VMEM((2, QCONV, 2 * ext, 128), f32),
            pltpu.VMEM((2, count, 256), bf),
            pltpu.VMEM((2, count, 128), f32),
        ]

    def cost(n):
        return pl.CostEstimate(
            flops=int(n * 1_500_000_000),
            bytes_accessed=int(n * 6_000_000),
            transcendentals=int(n * 300_000),
        )

    some_weights = on_chip((2, half, part), bf)
    span = on_chip((9 * rows, half), bf)
    e_src = pl.pallas_call(
        far_source_kernel,
        out_shape=on_chip((2 * rows, half), bf),
        in_specs=[vm, vm],
        out_specs=vm,
        compiler_params=small,
    )(own_kv, swap)
    last = lax.ppermute(e_src, "pb", far)
    qs, ks, vs, peak, total, acc = pl.pallas_call(
        own_kernel,
        out_shape=(on_chip((n_ext, half), bf), span, span)
        + state(on_chip)
,
        in_specs=[vm] * 6,
        out_specs=(vm,) * 6,
        scratch_shapes=work(n_rows),
        compiler_params=params,
        cost_estimate=cost(1),
    )(own_q, own_kv, swap, w, start, same)
    qs, ks, vs, peak, total, acc = pl.pallas_call(
        next_kernel,
        out_shape=(on_chip((n_ext, half), bf), span, span) + state(on_chip),
        in_specs=[vm] * 11,
        out_specs=(vm,) * 6,
        input_output_aliases={5: 0, 6: 1, 7: 2, 8: 3, 9: 4, 10: 5},
        scratch_shapes=work(n_rows),
        compiler_params=params,
        cost_estimate=cost(1),
    )(pa, pbk, w, start, same, qs, ks, vs, peak, total, acc)
    ks, vs, peak, total, acc = pl.pallas_call(
        mid_kernel,
        out_shape=(span, span) + state(on_chip),
        in_specs=[vm] * 11,
        out_specs=(vm,) * 5,
        input_output_aliases={6: 0, 7: 1, 8: 2, 9: 3, 10: 4},
        scratch_shapes=work(n_rows),
        compiler_params=params,
        cost_estimate=cost(1),
    )(fa, fb, w, start, same, qs, ks, vs, peak, total, acc)
    ends = [pltpu.VMEM((GROUP, rows, 128), f32), pltpu.VMEM((GROUP, rows, half), f32)]
    odd = pl.pallas_call(
        odd_kernel,
        out_shape=on_chip((rows, half), bf),
        in_specs=[vm] * 11,
        out_specs=vm,
        scratch_shapes=work(rows) + ends,
        compiler_params=params,
        cost_estimate=cost(0.5),
    )(blend, gain_own, w, start, same, qs, ks, vs, peak, total, acc)
    last, odd = lax.optimization_barrier((last, odd))
    mine, theirs, _, _ = pl.pallas_call(
        even_kernel,
        out_shape=(on_chip((rows, half), bf),) * 2 + (span, span),
        in_specs=[vm] * 13,
        out_specs=(vm,) * 4,
        input_output_aliases={8: 2, 9: 3},
        scratch_shapes=work(rows) + ends + [pltpu.VMEM((rows, half), bf)],
        compiler_params=params,
        cost_estimate=cost(0.5),
    )(blend, gain_own, odd, last, w, start, same, qs, ks, vs, peak, total, acc)
    got = lax.ppermute(theirs, "pb", swap_route)

    own_part, w_far = pl.pallas_call(
        own_part_kernel,
        out_shape=(on_chip((n_ha, rows, part), f32), some_weights),
        in_specs=[vm, vm, hbm],
        out_specs=(vm, vm),
        scratch_shapes=[pltpu.SemaphoreType.DMA((2,))],
        compiler_params=params,
        cost_estimate=pl.CostEstimate(
            flops=2 * rows * half * cols, bytes_accessed=8_000_000, transcendentals=0
        ),
    )(mine, w_own, heavy)
    halves = (on_chip((rows, part), bf), on_chip((rows, part), bf))
    half_cost = pl.CostEstimate(
        flops=rows * half * cols, bytes_accessed=4_000_000, transcendentals=0
    )

    near_route = [(i, i ^ 1) for i in range(n_ha)]

    def far_part(n):
        return pl.pallas_call(
            functools.partial(one_part_kernel, n=n),
            out_shape=halves[n],
            in_specs=[vm, vm, vm],
            out_specs=vm,
            compiler_params=params,
            cost_estimate=half_cost,
        )(got, w_far, own_part)

    give = far_part(0)
    keep = far_part(1)
    take = lax.ppermute(give, "ha", near_route)
    away = (keep.astype(f32) + take.astype(f32)).astype(bf)
    arrived = lax.ppermute(away, "ha", [(i, i ^ 2) for i in range(n_ha)])
    give, keep = pl.pallas_call(
        late_part_kernel,
        out_shape=halves,
        in_specs=[vm, hbm, vm],
        out_specs=(vm, vm),
        scratch_shapes=[pltpu.VMEM((2, half, part), bf), pltpu.SemaphoreType.DMA((2,))],
        compiler_params=params,
        cost_estimate=half_cost,
    )(got, heavy, own_part)
    take = lax.ppermute(give, "ha", near_route)
    here = keep.astype(f32) + take.astype(f32)
    return (here + arrived.astype(f32)).astype(bf)


def per_device(queries, keys, values, theta, mix, gain, out_weight, turn_lengths):
    rows, feats = queries.shape
    heads = theta.shape[0]
    fits = rows == 128 and feats == 128 * heads and heads == 2 * GROUP
    n_pb, n_ha = lax.axis_size("pb"), lax.axis_size("ha")
    fits = fits and n_pb % 2 == 0 and n_ha == 4
    args = (queries, keys, values, theta, mix, gain, out_weight, turn_lengths)
    if not fits:
        return general_plan(*args)
    return paired_plan(*args)


def solution(mesh):
    return jax.shard_map(
        per_device,
        mesh=mesh,
        in_specs=(
            P("pb", "ha"),
            P("pb", "ha"),
            P("pb", "ha"),
            P("ha", None, None),
            P("ha", None),
            P("ha"),
            P("ha", None),
            P(),
        ),
        out_specs=P("pb", "ha"),
        check_vma=False,
    )
```
